128 devices in a mesh: req: 4 (over z), exp: 32 (over x, y, core).
Axes of the slice: x: 4, y: 4, z: 4, core: 2. Of those that a mesh axis runs over, the one named last changes fastest.
Arguments:
- queries: bfloat16 [128, 64, 2048], P(('req', 'exp'))
- new_kv: bfloat16 [128, 64, 2, 2048], P(('req', 'exp')), may hold values from -6 to 6
- cache: bfloat16 [128, 512, 2, 2048], P(('req', 'exp'))
- lengths: int32 [128], P(('req', 'exp')), may hold values from 8 to 448
- residual: bfloat16 [128, 64, 2048], P(('req', 'exp')), may hold values from -6 to 6
- out_weight: bfloat16 [2048, 2048], replicated, may hold values from -0.125 to 0.125
- norm_gain: float32 [2048], replicated, may hold values from 0.1 to 1.9
- expert_ids: int32 [128, 64, 8], P(('req', 'exp')), may hold values from 0 to 63, all different within a row; in each aligned block of 64 rows (0 to 63, 64 to 127, ..., all dimensions but the last counted through in order) at most 10 rows name the same one
- gates: float32 [128, 64, 8], P(('req', 'exp')), may hold values from 0.1 to 1
- w_gate: bfloat16 [128, 2048, 512], P(('req', 'exp')), may hold values from -0.125 to 0.125
- w_up: bfloat16 [128, 2048, 512], P(('req', 'exp')), may hold values from -0.125 to 0.125
- w_down: bfloat16 [128, 512, 2048], P(('req', 'exp')), may hold values from -0.1875 to 0.1875
Outputs:
- layer_out: bfloat16 [128, 64, 2048], P(('req', 'exp'))
- appended: bfloat16 [128, 512, 2, 2048], P(('req', 'exp'))
The draws below stay inside these ranges and needn't reach their ends.
Inputs may be any that keep to these rules, and one draw needn't show every extreme that they name: `expert_ids`: among the tokens of one request, no expert is named by more than 10 rows.
All inputs are finite; a program needn't handle non-finite values.
Results may differ from the reference program's by a relative error of at most 0.0095.
Values may be sent and summed in bfloat16 or wider, within the bound.
A program may use at most 128 MiB of HBM per device.

```python
import math
import jax
import jax.numpy as jnp
import numpy as np
from jax import lax

D = 2048
HEADS = 16
HEAD_DIM = 128
FF = 1024
TOP = 8
GROUP = 64
CACHE = 512
REQS = 128
EXPERTS = 64
HALF = 512
CAP = 10


def cache_planes(key):
    key_plane = jax.random.normal(jax.random.fold_in(key, 11), (REQS, CACHE, D), jnp.float32)
    value_plane = jax.random.normal(jax.random.fold_in(key, 12), (REQS, CACHE, D), jnp.float32)
    nudged = jax.random.normal(jax.random.fold_in(key, 13), (REQS, D), jnp.float32)
    key_plane = key_plane.at[:, 1, :].set(key_plane[:, 0, :] + 0.15 * nudged)
    return (key_plane, value_plane)


def draw_cache(key, part):
    key_plane, value_plane = cache_planes(key)
    return jnp.stack([key_plane, value_plane], axis=2).astype(jnp.bfloat16)


def draw_queries(key, part):
    query_plane = jax.random.normal(jax.random.fold_in(key, 21), (REQS, GROUP, D), jnp.float32)
    return query_plane.astype(jnp.bfloat16)


def draw_lengths(key, part):
    spread = jax.random.randint(jax.random.fold_in(key, 31), (REQS,), 8, CACHE - GROUP + 1)
    shuffled = jax.random.permutation(jax.random.fold_in(key, 32), REQS)
    spread = jnp.where(shuffled == 0, CACHE - GROUP, spread)
    spread = jnp.where(shuffled == 1, 8, spread)
    return spread.astype(jnp.int32)


def steps_of(rng, extent, pieces, least, largest):
    factor_of, own = 1.0, jax.random.fold_in(rng, 6)
    for axis_at, blocks in pieces:
        heights = jnp.exp(jax.random.uniform(jax.random.fold_in(own, axis_at), (blocks,), jnp.float32, least / len(pieces), largest / len(pieces)))
        factor_of = factor_of * jnp.repeat(heights, extent[axis_at] // blocks).reshape([-1 if axis == axis_at else 1 for axis in range(len(extent))])
    return factor_of


def assign_block(key, own, number, rows, amount, top, bound, lean):
    order = jax.random.permutation(key, amount)
    crowded, common = load_shares(amount, rows * top, bound, lean, True), load_shares(amount, rows * top, bound, lean, False)
    places = jnp.arange(amount)

    def named(sizes, rotation):
        used = int((sizes > 0).sum())
        fixed = max(1, used // 4)
        moved = fixed + (places - fixed + rotation * (used - fixed)) % max(1, amount - fixed)
        return jnp.zeros((amount,), jnp.int32).at[order[jnp.where(places < fixed, places, moved)]].set(jnp.asarray(sizes, jnp.int32))

    sizes = jnp.where(number % 4 == 0, named(crowded, number // 4), named(common, number - number // 4 - 1))
    mixed = jax.random.permutation(jax.random.fold_in(own, 3), amount)
    donor, taker = mixed[0:amount // 2 * 2:2], mixed[1:amount // 2 * 2:2]
    room = jnp.minimum(sizes[donor] - 1, bound - sizes[taker]) // 2
    room = jnp.where((donor == order[0]) | (taker == order[0]) | (sizes[taker] == 0), 0, jnp.maximum(room, 0))
    moved = jax.random.randint(jax.random.fold_in(own, 4), (amount // 2,), 0, 1 << 20) % (room + 1)
    sizes = sizes.at[donor].add(-moved).at[taker].add(moved)
    members = jnp.searchsorted(jnp.cumsum(sizes), jnp.arange(rows * top), side="right").astype(jnp.int32)
    grid = members.reshape(top, rows).T
    grid = grid[jax.random.permutation(jax.random.fold_in(own, 1), rows)]
    rotation = jax.random.randint(jax.random.fold_in(own, 2), (rows, 1), 0, top)
    return jnp.take_along_axis(grid, (jnp.arange(top)[None, :] + rotation) % top, axis=1)


def load_shares(count, total, most, lean, full):
    loads = [(1 << 20) // math.isqrt(standing ** lean) + 1 for standing in range(1, count + 1)]
    largest = most if full else min(most, max(-(-total // count), total * loads[0] // sum(loads)))
    least = 1 if total - largest >= count - 1 else 0
    given, spare = [largest] + [least] * (count - 1), total - largest - least * (count - 1)
    while spare > 0:
        movable = [i for i in range(1, count) if given[i] < largest] or [i for i in range(1, count) if given[i] < most]
        pool, budget = sum([loads[i] for i in movable]), spare
        for i in movable:
            more = min(most - given[i], max(1, budget * loads[i] // pool), spare)
            given[i] = given[i] + more
            spare = spare - more
    return np.array(given)


def centred(key, extent, deviation, bound, cuts=(), kind=jnp.bfloat16):
    drawn = deviation * jax.random.normal(key, extent, jnp.float32)
    if cuts:
        drawn = drawn * steps_of(key, extent, cuts, -0.22, 0.18)
    return jnp.clip(drawn, -bound, bound).astype(kind)


def setup_inputs(seed: int = 0) -> dict:
    streams_of = jax.random.split(jax.random.key(seed), 13)
    queries = draw_queries(jax.random.fold_in(streams_of[12], 71), 0)
    new_kv = centred(streams_of[1], (REQS, GROUP, 2, D), 1.0, 6.0, ((0, 128),))
    cache = draw_cache(jax.random.fold_in(streams_of[12], 71), 0)
    lengths = draw_lengths(jax.random.fold_in(streams_of[12], 71), 0)
    residual = centred(streams_of[4], (REQS, GROUP, D), 1.0, 6.0, ((0, 128),))
    out_weight = centred(streams_of[5], (D, D), D ** -0.5, 0.125)
    norm_gain = jnp.clip(1.0 + 0.18 * jax.random.normal(streams_of[6], (D,), jnp.float32), 0.1, 1.9)
    expert_ids_keys = jax.random.split(jax.random.fold_in(streams_of[7], 1), REQS * GROUP // GROUP)
    expert_ids_turns = jax.random.permutation(jax.random.fold_in(streams_of[7], 3), REQS * GROUP // GROUP)
    expert_ids = jax.vmap(lambda own, number: assign_block(jax.random.fold_in(streams_of[7], 2), own, number, GROUP, EXPERTS, TOP, CAP, 1))(expert_ids_keys, expert_ids_turns).reshape((REQS, GROUP, TOP))
    gates = jnp.clip(0.1 + 0.9 * jax.random.uniform(streams_of[8], (REQS, GROUP, TOP), jnp.float32) ** steps_of(streams_of[8], (REQS, GROUP, TOP), ((0, 128),), -0.2, 0.2), 0.1, 1.0)
    w_gate = centred(streams_of[9], (2 * EXPERTS, D, HALF), D ** -0.5, 0.125, ((0, 128),))
    w_up = centred(streams_of[10], (2 * EXPERTS, D, HALF), D ** -0.5, 0.125, ((0, 128),))
    w_down = centred(streams_of[11], (2 * EXPERTS, HALF, D), FF ** -0.5, 0.1875, ((0, 128),))
    return dict(queries=queries, new_kv=new_kv, cache=cache, lengths=lengths, residual=residual, out_weight=out_weight, norm_gain=norm_gain, expert_ids=expert_ids, gates=gates, w_gate=w_gate, w_up=w_up, w_down=w_down)


masked_value = -1e+30

def attend_request(query_rows, new_rows, cache_rows, length_now, residual_rows, out_weight):
    key_rows = jnp.concatenate([cache_rows[:, 0], new_rows[:, 0]], axis=0)
    value_rows = jnp.concatenate([cache_rows[:, 1], new_rows[:, 1]], axis=0)
    positions = key_rows.shape[0]
    queried = query_rows.reshape(GROUP, HEADS, HEAD_DIM).astype(jnp.float32)
    keyed = key_rows.reshape(positions, HEADS, HEAD_DIM).astype(jnp.float32)
    valued = value_rows.reshape(positions, HEADS, HEAD_DIM).astype(jnp.float32)
    scores = jnp.einsum('qhd,khd->hqk', queried, keyed) * HEAD_DIM ** (-0.5)
    slot_place = jnp.arange(positions, dtype=jnp.int32)
    counted = (slot_place < length_now) | (slot_place >= CACHE)
    scores = jnp.where(counted[None, None, :], scores, masked_value)
    peak_score = lax.optimization_barrier(jnp.max(scores, axis=-1, keepdims=True))
    raised = jnp.exp(scores - peak_score)
    softmax_bf = (raised / lax.optimization_barrier(jnp.sum(raised, axis=-1, keepdims=True))).astype(jnp.bfloat16)
    mixed_heads = jnp.einsum('hqk,khd->qhd', softmax_bf.astype(jnp.float32), valued)
    attention = mixed_heads.reshape(GROUP, HEADS * HEAD_DIM).astype(jnp.bfloat16)
    stream = residual_rows.astype(jnp.float32) + jnp.dot(attention, out_weight, preferred_element_type=jnp.float32)
    start_at = length_now.astype(jnp.int32)
    appended = lax.dynamic_update_slice(cache_rows, new_rows, (start_at, jnp.int32(0), jnp.int32(0)))
    return (stream, appended)

def reference(queries, new_kv, cache, lengths, residual, out_weight, norm_gain, expert_ids, gates, w_gate, w_up, w_down):

    def per_request(packed):
        return attend_request(packed[0], packed[1], packed[2], packed[3], packed[4], out_weight)
    stream, appended = lax.map(per_request, (queries, new_kv, cache, lengths, residual))
    mean_square = lax.optimization_barrier(jnp.mean(stream * stream, axis=-1, keepdims=True))
    normed = (stream * lax.rsqrt(mean_square + 1e-06) * norm_gain).astype(jnp.bfloat16)
    flat_rows = jnp.concatenate([normed.reshape(REQS * GROUP, D), jnp.zeros((1, D), jnp.bfloat16)], axis=0)
    routed = expert_ids.reshape(REQS, GROUP * TOP)
    weights_flat = gates.reshape(-1)
    row_token = jnp.arange(REQS * GROUP * TOP, dtype=jnp.int32) // TOP
    block_base = jnp.arange(REQS, dtype=jnp.int32)[:, None] * CAP

    def expert_step(accumulated, expert):
        hit_mask = (routed == expert).astype(jnp.int32)
        ranking = jnp.cumsum(hit_mask, axis=1) - hit_mask
        slot_index = jnp.where(hit_mask == 1, block_base + ranking, REQS * CAP).reshape(-1)
        token_of = jnp.full((REQS * CAP,), REQS * GROUP, jnp.int32).at[slot_index].set(row_token, mode='drop')
        gate_of = jnp.zeros((REQS * CAP,), weights_flat.dtype).at[slot_index].set(weights_flat, mode='drop')
        picked_rows = flat_rows[token_of]
        gate_full = jnp.concatenate([w_gate[2 * expert], w_gate[2 * expert + 1]], axis=1)
        up_full = jnp.concatenate([w_up[2 * expert], w_up[2 * expert + 1]], axis=1)
        down_full = jnp.concatenate([w_down[2 * expert], w_down[2 * expert + 1]], axis=0)
        gate_act = jnp.dot(picked_rows, gate_full, preferred_element_type=jnp.float32)
        up_act = jnp.dot(picked_rows, up_full, preferred_element_type=jnp.float32)
        hidden = (jax.nn.silu(gate_act) * up_act).astype(jnp.bfloat16)
        expert_out = jnp.dot(hidden, down_full, preferred_element_type=jnp.float32).astype(jnp.bfloat16)
        accumulated = accumulated.at[token_of].add(gate_of[:, None] * expert_out.astype(accumulated.dtype), mode='drop')
        return (accumulated, None)
    start_sum = jnp.zeros((REQS * GROUP, D), stream.dtype)
    blended, _ = lax.scan(expert_step, start_sum, jnp.arange(EXPERTS, dtype=jnp.int32))
    layer_out = (stream.reshape(REQS * GROUP, D) + blended).astype(jnp.bfloat16).reshape(REQS, GROUP, D)
    return (layer_out, appended)
```

```python
import functools

import jax
import jax.numpy as jnp
from jax import lax
from jax.experimental import pallas as pl
from jax.experimental.pallas import tpu as pltpu
from jax.sharding import PartitionSpec as P

MESH = pl.DeviceIdType.MESH
F32 = jnp.float32
BF16 = jnp.bfloat16

GROUP = 64
D = 2048
HEADS = 16
HEAD_DIM = 128
EXPERTS = 64
TOP = 8
HALF = 512
CAP = 10
CACHE = 512
SEEN = 448
LANES = 128
PIECES = D // LANES
CHUNKS = 4
PEERS = EXPERTS // CHUNKS
ROWS = PEERS * CAP
MASKED = -1e30


def dot(a, b, dims=((1,), (0,))):
    return lax.dot_general(a, b, (dims, ((), ())), preferred_element_type=F32)


def offsets(i):
    dx, dy = (i // 4) % 4, i % 4
    return (i // PEERS + 8 - dx - dy) % 4, dx, dy


def layer_kernel(
    length_ref,
    ids_ref,
    gates_ref,
    gain_ref,
    q_hbm,
    kv_hbm,
    cache_hbm,
    res_hbm,
    ow_hbm,
    wg_hbm,
    wu_hbm,
    wd_hbm,
    out_ref,
    q_ref,
    kv_ref,
    res_ref,
    ow_ref,
    wg_ref,
    wu_ref,
    wd_ref,
    att_ref,
    stream_ref,
    normed_ref,
    pick_ref,
    mixhi_ref,
    mixlo_ref,
    wide_ref,
    x_ref,
    h_ref,
    out_rows,
    in_rows,
    done_rows,
    back_rows,
    local_sem,
    mate_send,
    mate_recv,
    send_sem,
    recv_sem,
    back_send,
    back_recv,
):
    z = lax.axis_index("req")
    along = lax.axis_index("exp")
    core = along % 2
    x = along // 8
    y = (along // 2) % 4

    def device(i, sign):
        dz, dx, dy = offsets(i)
        there = (((x + sign * dx + 4) % 4) * 4 + (y + sign * dy + 4) % 4) * 2 + core
        return {"req": (z + sign * dz + 4) % 4, "exp": there}

    mate = {"req": z, "exp": along + 1 - 2 * core}

    barrier = pltpu.get_barrier_semaphore()

    def greet(i, carry):
        pl.semaphore_signal(barrier, inc=1, device_id=device(i, 1), device_id_type=MESH)
        return carry

    lax.fori_loop(1, EXPERTS, greet, 0)
    pl.semaphore_signal(barrier, inc=1, device_id=mate, device_id_type=MESH)

    loads = [
        pltpu.make_async_copy(cache_hbm.at[pl.ds(0, SEEN)], kv_ref.at[pl.ds(0, SEEN)], local_sem.at[0]),
        pltpu.make_async_copy(kv_hbm, kv_ref.at[pl.ds(SEEN, GROUP)], local_sem.at[1]),
        pltpu.make_async_copy(q_hbm, q_ref, local_sem.at[2]),
        pltpu.make_async_copy(res_hbm, res_ref, local_sem.at[3]),
        pltpu.make_async_copy(ow_hbm, ow_ref, local_sem.at[4]),
        pltpu.make_async_copy(wg_hbm, wg_ref.at[core], local_sem.at[5]),
        pltpu.make_async_copy(wu_hbm, wu_ref.at[core], local_sem.at[6]),
        pltpu.make_async_copy(wd_hbm, wd_ref.at[core], local_sem.at[7]),
    ]
    for copy in (loads[2], loads[1], loads[0], loads[3], loads[4]):
        copy.start()
    for copy in loads[5:]:
        copy.start()
    swaps = [
        pltpu.make_async_remote_copy(
            src_ref=src, dst_ref=dst.at[core], send_sem=mate_send.at[k], recv_sem=mate_recv.at[k],
            device_id=mate, device_id_type=MESH,
        )
        for k, (src, dst) in enumerate(((wg_hbm, wg_ref), (wu_hbm, wu_ref), (wd_hbm, wd_ref)))
    ]

    expert_of = lax.broadcasted_iota(jnp.int32, (EXPERTS, GROUP), 0)
    hit = jnp.zeros((EXPERTS, GROUP), F32)
    gate_of = jnp.zeros((EXPERTS, GROUP), F32)
    for k in range(TOP):
        same = ids_ref[k : k + 1, :] == expert_of
        hit = jnp.where(same, 1.0, hit)
        gate_of = jnp.where(same, gates_ref[k : k + 1, :], gate_of)
    t_row = lax.broadcasted_iota(jnp.int32, (GROUP, GROUP), 0)
    t_col = lax.broadcasted_iota(jnp.int32, (GROUP, GROUP), 1)
    before = jnp.where(t_row < t_col, 1.0, 0.0).astype(BF16)
    eye = jnp.where(t_row == t_col, 1.0, 0.0).astype(BF16)
    rank = dot(hit.astype(BF16), before)
    rank = jnp.where(hit > 0.5, rank, 99.0).astype(BF16)
    gate_hi = gate_of.astype(BF16)
    gate_lo = (gate_of - gate_hi.astype(F32)).astype(BF16)

    def slots(shape, axis):
        row = lax.broadcasted_iota(jnp.int32, shape, axis)
        i = (row * 6554) >> 16
        dx, dy = (i >> 2) & 3, i & 3
        dz = ((i >> 4) + 8 - dx - dy) & 3
        expert = (((z + dz) & 3) << 4) + (((x + dx) & 3) << 2) + ((y + dy) & 3)
        return (row - i * CAP).astype(F32), expert

    slot, expert = slots((EXPERTS * CAP, EXPERTS), 0)
    spread = jnp.where(expert == lax.broadcasted_iota(jnp.int32, expert.shape, 1), 1.0, 0.0).astype(BF16)
    pick_ref[...] = jnp.where(dot(spread, rank) == slot, 1.0, 0.0).astype(BF16)
    slot, expert = slots((EXPERTS, EXPERTS * CAP), 1)
    spread = jnp.where(expert == lax.broadcasted_iota(jnp.int32, expert.shape, 0), 1.0, 0.0).astype(BF16)
    turned = ((1,), (1,))
    chosen = dot(dot(eye, rank, turned).astype(BF16), spread) == slot
    for table, part in ((mixhi_ref, gate_hi), (mixlo_ref, gate_lo)):
        spread_gate = dot(dot(eye, part, turned).astype(BF16), spread)
        whole = jnp.where(chosen, spread_gate, 0.0).astype(BF16)
        for j in range(CHUNKS):
            table[j] = whole[:, j * ROWS : (j + 1) * ROWS]

    for copy in (loads[2], loads[1], loads[0]):
        copy.wait()
    column = lax.broadcasted_iota(jnp.int32, (GROUP, 2 * (SEEN + GROUP)), 1)
    place = column >> 1
    length = length_ref[0]
    counted = ((column & 1) == 0) & ((place < length) | (place >= SEEN))

    def head(h, carry):
        at = pl.ds(pl.multiple_of(h * HEAD_DIM, HEAD_DIM), HEAD_DIM)
        pairs = kv_ref[:, :, at].reshape(2 * (SEEN + GROUP), HEAD_DIM)
        scores = dot(q_ref[:, at], pairs, ((1,), (1,))) * HEAD_DIM ** (-0.5)
        scores = jnp.where(counted, scores, MASKED)
        raised = jnp.exp(scores - jnp.max(scores, axis=1, keepdims=True))
        share = raised / jnp.sum(raised, axis=1, keepdims=True)
        share = pltpu.roll(share, 1, 1).astype(BF16)
        att_ref[:, at] = dot(share, pairs).astype(BF16)
        return carry

    lax.fori_loop(0, HEADS // 2, head, 0)
    pl.semaphore_wait(barrier, EXPERTS)
    for swap in swaps:
        swap.start()
    lax.fori_loop(HEADS // 2, HEADS, head, 0)

    for copy in loads[3:5]:
        copy.wait()

    def project(n, carry):
        at = pl.ds(pl.multiple_of(n * 256, 256), 256)
        stream_ref[:, at] = res_ref[:, at].astype(F32) + dot(att_ref[...], ow_ref[:, at])
        return carry

    lax.fori_loop(0, D // 256, project, 0)
    stream = stream_ref[...]
    mean_square = jnp.mean(stream * stream, axis=1, keepdims=True)
    normed_ref[...] = (stream * lax.rsqrt(mean_square + 1e-06) * gain_ref[...]).astype(BF16)

    def send_copy(i):
        return pltpu.make_async_remote_copy(
            src_ref=out_rows.at[i], dst_ref=in_rows.at[i], send_sem=send_sem.at[i], recv_sem=recv_sem.at[i],
            device_id=device(i, 1), device_id_type=MESH,
        )

    def back_copy(i):
        return pltpu.make_async_remote_copy(
            src_ref=done_rows.at[i], dst_ref=back_rows.at[i], send_sem=back_send.at[i], recv_sem=back_recv.at[i],
            device_id=device(i, -1), device_id_type=MESH,
        )

    own_out = pltpu.make_async_copy(out_rows.at[0], in_rows.at[0], recv_sem.at[0])
    own_back = pltpu.make_async_copy(done_rows.at[0], back_rows.at[0], back_recv.at[0])

    def tiles_out(rows, j):
        rows[pl.ds(j * PEERS, PEERS)] = wide_ref[...].reshape(PEERS, CAP, PIECES, LANES).astype(BF16)

    def tiles_in(rows, j):
        wide_ref[...] = rows[pl.ds(j * PEERS, PEERS)].astype(F32).reshape(ROWS * PIECES, LANES)
        for c in range(PIECES):
            x_ref[:, c * LANES : (c + 1) * LANES] = wide_ref[pl.ds(c, ROWS, stride=PIECES), :].astype(BF16)

    def each_peer(j, action):
        def body(i, carry):
            action(i)
            return carry

        lax.fori_loop(j * PEERS + (1 if j == 0 else 0), (j + 1) * PEERS, body, 0)

    for j in range(CHUNKS):
        picked = pick_ref[j * ROWS : (j + 1) * ROWS, :]
        for c in range(PIECES):
            wide_ref[pl.ds(c, ROWS, stride=PIECES), :] = dot(picked, normed_ref[:, c * LANES : (c + 1) * LANES])
        tiles_out(out_rows, j)
        if j == 0:
            own_out.start()
        each_peer(j, lambda i: send_copy(i).start())

    for copy in loads[5:]:
        copy.wait()
    for swap in swaps:
        swap.wait()

    for j in range(CHUNKS):
        if j == 0:
            own_out.wait()
        each_peer(j, lambda i: send_copy(i).wait_recv())
        tiles_in(in_rows, j)

        def hidden(n, carry):
            half, at = n // 2, pl.ds(pl.multiple_of((n % 2) * 256, 256), 256)
            gate = dot(x_ref[...], wg_ref[half, :, at])
            up = dot(x_ref[...], wu_ref[half, :, at])
            h_ref[:, pl.ds(pl.multiple_of(n * 256, 256), 256)] = (gate / (1.0 + jnp.exp(-gate)) * up).astype(BF16)
            return carry

        lax.fori_loop(0, 4, hidden, 0)

        def down(n, carry):
            at = pl.ds(pl.multiple_of(n * 256, 256), 256)
            rows = dot(h_ref[:, :HALF], wd_ref[0, :, at]) + dot(h_ref[:, HALF:], wd_ref[1, :, at])
            wide_ref[pl.ds(2 * n, ROWS, stride=PIECES), :] = rows[:, :LANES]
            wide_ref[pl.ds(2 * n + 1, ROWS, stride=PIECES), :] = rows[:, LANES:]
            return carry

        lax.fori_loop(0, D // 256, down, 0)
        tiles_out(done_rows, j)
        if j == 0:
            own_back.start()
        each_peer(j, lambda i: back_copy(i).start())

    for j in range(CHUNKS):
        if j == 0:
            own_back.wait()
        each_peer(j, lambda i: back_copy(i).wait_recv())
        tiles_in(back_rows, j)
        for n in range(D // 512):
            at = slice(n * 512, (n + 1) * 512)
            stream_ref[:, at] += dot(mixhi_ref[j], x_ref[:, at]) + dot(mixlo_ref[j], x_ref[:, at])
    out_ref[...] = stream_ref[...].astype(BF16)

    for j in range(CHUNKS):
        each_peer(j, lambda i: send_copy(i).wait_send())
        each_peer(j, lambda i: back_copy(i).wait_send())


def append_kernel(length_ref, kv_hbm, cache_hbm, out_hbm, held, new, in_sem, out_sem):
    pieces = 8
    size = CACHE // pieces
    parts = [pl.ds(k * size, size) for k in range(pieces)]
    ins = [pltpu.make_async_copy(cache_hbm.at[p], held.at[p], in_sem.at[k]) for k, p in enumerate(parts)]
    outs = [pltpu.make_async_copy(held.at[p], out_hbm.at[p], out_sem.at[k]) for k, p in enumerate(parts)]
    fetch = pltpu.make_async_copy(kv_hbm, new, in_sem.at[pieces])
    for copy in ins:
        copy.start()
    fetch.start()
    for arrive, leave in zip(ins, outs):
        arrive.wait()
        leave.start()
    fetch.wait()
    for leave in outs:
        leave.wait()
    write = pltpu.make_async_copy(new, out_hbm.at[pl.ds(length_ref[0], GROUP)], out_sem.at[pieces])
    write.start()
    write.wait()


def shards(
    queries, new_kv, cache, lengths, residual, out_weight, norm_gain, expert_ids, gates, w_gate, w_up, w_down
):
    anywhere = pl.BlockSpec(memory_space=pl.ANY)
    in_vmem = pl.BlockSpec(memory_space=pltpu.VMEM)
    in_smem = pl.BlockSpec(memory_space=pltpu.SMEM)
    tiles = (EXPERTS, CAP, PIECES, LANES)
    layer_out = pl.pallas_call(
        layer_kernel,
        name="layer",
        out_shape=jax.ShapeDtypeStruct((GROUP, D), BF16),
        in_specs=[in_smem, in_vmem, in_vmem, in_vmem] + [anywhere] * 8,
        out_specs=in_vmem,
        scratch_shapes=[
            pltpu.VMEM((GROUP, D), BF16),
            pltpu.VMEM((SEEN + GROUP, 2, D), BF16),
            pltpu.VMEM((GROUP, D), BF16),
            pltpu.VMEM((D, D), BF16),
            pltpu.VMEM((2, D, HALF), BF16),
            pltpu.VMEM((2, D, HALF), BF16),
            pltpu.VMEM((2, HALF, D), BF16),
            pltpu.VMEM((GROUP, D), BF16),
            pltpu.VMEM((GROUP, D), F32),
            pltpu.VMEM((GROUP, D), BF16),
            pltpu.VMEM((EXPERTS * CAP, GROUP), BF16),
            pltpu.VMEM((CHUNKS, GROUP, ROWS), BF16),
            pltpu.VMEM((CHUNKS, GROUP, ROWS), BF16),
            pltpu.VMEM((ROWS * PIECES, LANES), F32),
            pltpu.VMEM((ROWS, D), BF16),
            pltpu.VMEM((ROWS, 2 * HALF), BF16),
            pltpu.VMEM(tiles, BF16),
            pltpu.VMEM(tiles, BF16),
            pltpu.VMEM(tiles, BF16),
            pltpu.VMEM(tiles, BF16),
            pltpu.SemaphoreType.DMA((8,)),
            pltpu.SemaphoreType.DMA((3,)),
            pltpu.SemaphoreType.DMA((3,)),
            pltpu.SemaphoreType.DMA((EXPERTS,)),
            pltpu.SemaphoreType.DMA((EXPERTS,)),
            pltpu.SemaphoreType.DMA((EXPERTS,)),
            pltpu.SemaphoreType.DMA((EXPERTS,)),
        ],
        compiler_params=pltpu.CompilerParams(
            collective_id=0, has_side_effects=True, vmem_limit_bytes=60 * 1024 * 1024
        ),
    )(
        lengths,
        expert_ids[0].T,
        gates[0].T,
        norm_gain[None],
        queries[0],
        new_kv[0],
        cache[0],
        residual[0],
        out_weight,
        w_gate[0],
        w_up[0],
        w_down[0],
    )
    appended = pl.pallas_call(
        append_kernel,
        name="append",
        out_shape=jax.ShapeDtypeStruct((CACHE, 2, D), BF16),
        in_specs=[in_smem, anywhere, anywhere],
        out_specs=anywhere,
        scratch_shapes=[
            pltpu.VMEM((CACHE, 2, D), BF16),
            pltpu.VMEM((GROUP, 2, D), BF16),
            pltpu.SemaphoreType.DMA((9,)),
            pltpu.SemaphoreType.DMA((9,)),
        ],
    )(lengths, new_kv[0], cache[0])
    return layer_out[None], appended[None]


def solution(mesh):
    shared = ("req", "exp")
    three, four = P(shared, None, None), P(shared, None, None, None)
    return jax.shard_map(
        shards,
        mesh=mesh,
        in_specs=(three, four, four, P(shared), three, P(), P(), three, three, three, three, three),
        out_specs=(three, four),
        check_vma=False,
    )
```

```python
import math

import jax
import jax.numpy as jnp
from jax import lax
from jax.experimental import pallas as pl
from jax.experimental.pallas import tpu as pltpu
from jax.sharding import PartitionSpec as P

MESH = pl.DeviceIdType.MESH
F32 = jnp.float32
BF16 = jnp.bfloat16

GROUP = 64
D = 2048
HEADS = 16
HEAD_DIM = 128
EXPERTS = 64
TOP = 8
HALF = 512
CAP = 10
CACHE = 512
SEEN = 448
LANES = 128
PIECES = D // LANES
CHUNKS = 4
PEERS = EXPERTS // CHUNKS
ROWS = PEERS * CAP
MASKED = -1e30 * HEAD_DIM**0.5
AHEAD = 2
GROUPS = 4
STEP = 16
WIDE = D // GROUPS
PAIRS = 2 * (SEEN + GROUP)
SCALE = HEAD_DIM ** (-0.5) / math.log(2.0)


def dot(a, b, dims=((1,), (0,))):
    return lax.dot_general(a, b, (dims, ((), ())), preferred_element_type=F32)


def offsets(i):
    dx, dy = (i // 4) % 4, i % 4
    return (i // PEERS + 8 - dx - dy) % 4, dx, dy


def layer_kernel(
    length_hbm,
    ids_hbm,
    gates_hbm,
    gain_hbm,
    q_hbm,
    keys_ref,
    values_ref,
    res_hbm,
    ow_hbm,
    wg_hbm,
    wu_hbm,
    wd_hbm,
    out_ref,
    length_ref,
    keep_ref,
    ids_ref,
    gates_ref,
    gain_ref,
    q_ref,
    res_ref,
    ow_ref,
    wg_ref,
    wu_ref,
    wd_ref,
    att_ref,
    stream_ref,
    normed_ref,
    pick_ref,
    mixhi_ref,
    mixlo_ref,
    wide_ref,
    x_ref,
    h_ref,
    out_rows,
    in_rows,
    done_rows,
    back_rows,
    local_sem,
    ow_sem,
    mate_send,
    mate_recv,
    send_sem,
    recv_sem,
    back_send,
    back_recv,
):
    z = lax.axis_index("req")
    along = lax.axis_index("exp")
    core = along % 2
    x = along // 8
    y = (along // 2) % 4

    def device(i, sign):
        dz, dx, dy = offsets(i)
        there = (((x + sign * dx + 4) % 4) * 4 + (y + sign * dy + 4) % 4) * 2 + core
        return {"req": (z + sign * dz + 4) % 4, "exp": there}

    mate = {"req": z, "exp": along + 1 - 2 * core}

    small = [
        pltpu.make_async_copy(q_hbm, q_ref, local_sem.at[0]),
        pltpu.make_async_copy(length_hbm, length_ref, local_sem.at[1]),
        pltpu.make_async_copy(res_hbm, res_ref, local_sem.at[2]),
        pltpu.make_async_copy(gain_hbm, gain_ref, local_sem.at[6]),
    ]
    tables = [
        pltpu.make_async_copy(ids_hbm, ids_ref, local_sem.at[7]),
        pltpu.make_async_copy(gates_hbm, gates_ref, local_sem.at[8]),
    ]
    weights = [
        pltpu.make_async_copy(wg_hbm, wg_ref.at[core], local_sem.at[3]),
        pltpu.make_async_copy(wu_hbm, wu_ref.at[core], local_sem.at[4]),
        pltpu.make_async_copy(wd_hbm, wd_ref.at[core], local_sem.at[5]),
    ]

    def ow_copy(g):
        at = pl.ds(pl.multiple_of(g * WIDE, WIDE), WIDE)
        return pltpu.make_async_copy(ow_hbm.at[at], ow_ref.at[at], ow_sem.at[g])

    for copy in tables + small:
        copy.start()

    for g in range(GROUPS):
        ow_copy(g).start()
    barrier = pltpu.get_barrier_semaphore()

    def greet(i, carry):
        pl.semaphore_signal(barrier, inc=1, device_id=device(i, 1), device_id_type=MESH)
        return carry

    lax.fori_loop(1, EXPERTS, greet, 0)
    pl.semaphore_signal(barrier, inc=1, device_id=mate, device_id_type=MESH)

    swaps = [
        pltpu.make_async_remote_copy(
            src_ref=src, dst_ref=dst.at[core], send_sem=mate_send.at[k], recv_sem=mate_recv.at[k],
            device_id=mate, device_id_type=MESH,
        )
        for k, (src, dst) in enumerate(((wg_hbm, wg_ref), (wu_hbm, wu_ref), (wd_hbm, wd_ref)))
    ]

    for copy in tables:
        copy.wait()

    expert_of = lax.broadcasted_iota(jnp.int32, (EXPERTS, GROUP), 0)
    hit = jnp.zeros((EXPERTS, GROUP), F32)
    gate_of = jnp.zeros((EXPERTS, GROUP), F32)
    for k in range(TOP):
        same = ids_ref[k : k + 1, :] == expert_of
        hit = jnp.where(same, 1.0, hit)
        gate_of = jnp.where(same, gates_ref[k : k + 1, :], gate_of)
    t_row = lax.broadcasted_iota(jnp.int32, (GROUP, GROUP), 0)
    t_col = lax.broadcasted_iota(jnp.int32, (GROUP, GROUP), 1)
    before = jnp.where(t_row < t_col, 1.0, 0.0).astype(BF16)
    eye = jnp.where(t_row == t_col, 1.0, 0.0).astype(BF16)
    rank = dot(hit.astype(BF16), before)
    rank = jnp.where(hit > 0.5, rank, 99.0).astype(BF16)
    gate_hi = gate_of.astype(BF16)
    gate_lo = (gate_of - gate_hi.astype(F32)).astype(BF16)

    def slots(shape, axis):
        row = lax.broadcasted_iota(jnp.int32, shape, axis)
        i = (row * 6554) >> 16
        dx, dy = (i >> 2) & 3, i & 3
        dz = ((i >> 4) + 8 - dx - dy) & 3
        expert = (((z + dz) & 3) << 4) + (((x + dx) & 3) << 2) + ((y + dy) & 3)
        return (row - i * CAP).astype(F32), expert

    slot, expert = slots((EXPERTS * CAP, EXPERTS), 0)
    spread = jnp.where(expert == lax.broadcasted_iota(jnp.int32, expert.shape, 1), 1.0, 0.0).astype(BF16)
    pick_ref[...] = jnp.where(dot(spread, rank) == slot, 1.0, 0.0).astype(BF16)
    for copy in small:
        copy.wait()
    place = lax.broadcasted_iota(jnp.int32, (8, SEEN + GROUP), 1)
    length = length_ref[0]
    keep_ref[...] = jnp.where((place < length) | (place >= SEEN), 1.0, 0.0)

    def head(h):
        at = pl.ds(pl.multiple_of(h * HEAD_DIM, HEAD_DIM), HEAD_DIM)
        scores = dot(q_ref[:, at], keys_ref[h], ((1,), (1,)))
        scores = jnp.where(keep_ref[0:1, :] > 0.5, scores, MASKED)
        raised = jnp.exp2((scores - jnp.max(scores, axis=1, keepdims=True)) * SCALE)
        total = jnp.sum(raised, axis=1, keepdims=True)
        att_ref[:, at] = (dot(raised.astype(BF16), values_ref[h]) / total).astype(BF16)

    def group(g, carry):
        heads = [g * (HEADS // GROUPS) + k for k in range(HEADS // GROUPS)]
        for h in heads:
            head(h)
        ow_copy(g).wait()
        at = pl.ds(pl.multiple_of(g * WIDE, WIDE), WIDE)
        for n in range(0, D, 512):
            stream_ref[:, n : n + 512] += dot(att_ref[:, at], ow_ref[at, n : n + 512])
        return carry

    stream_ref[...] = res_ref[...].astype(F32)
    lax.fori_loop(0, 1, group, 0)
    pl.semaphore_wait(barrier, EXPERTS)
    for swap in swaps:
        swap.start()
    lax.fori_loop(1, GROUPS, group, 0)
    for copy in weights:
        copy.start()

    stream = stream_ref[...]
    mean_square = jnp.mean(stream * stream, axis=1, keepdims=True)
    normed_ref[...] = (stream * lax.rsqrt(mean_square + 1e-06) * gain_ref[...]).astype(BF16)

    def send_copy(i):
        return pltpu.make_async_remote_copy(
            src_ref=out_rows.at[i], dst_ref=in_rows.at[i], send_sem=send_sem.at[i], recv_sem=recv_sem.at[i],
            device_id=device(i, 1), device_id_type=MESH,
        )

    def back_copy(i):
        return pltpu.make_async_remote_copy(
            src_ref=done_rows.at[i], dst_ref=back_rows.at[i], send_sem=back_send.at[i], recv_sem=back_recv.at[i],
            device_id=device(i, -1), device_id_type=MESH,
        )

    own_out = pltpu.make_async_copy(out_rows.at[0], in_rows.at[0], recv_sem.at[0])
    own_back = pltpu.make_async_copy(done_rows.at[0], back_rows.at[0], back_recv.at[0])

    def tiles_out(rows, j):
        rows[pl.ds(j * PEERS, PEERS)] = wide_ref[...].reshape(PEERS, CAP, PIECES, LANES).astype(BF16)

    def tiles_in(rows, j):
        wide_ref[...] = rows[pl.ds(j * PEERS, PEERS)].astype(F32).reshape(ROWS * PIECES, LANES)
        for c in range(PIECES):
            x_ref[:, c * LANES : (c + 1) * LANES] = wide_ref[pl.ds(c, ROWS, stride=PIECES), :].astype(BF16)

    def each_peer(j, action):
        def body(i, carry):
            action(i)
            return carry

        lax.fori_loop(j * PEERS + (1 if j == 0 else 0), (j + 1) * PEERS, body, 0)

    def send(j):
        picked = pick_ref[j * ROWS : (j + 1) * ROWS, :]
        for c in range(PIECES):
            wide_ref[pl.ds(c, ROWS, stride=PIECES), :] = dot(picked, normed_ref[:, c * LANES : (c + 1) * LANES])
        tiles_out(out_rows, j)
        if j == 0:
            own_out.start()
        each_peer(j, lambda i: send_copy(i).start())

    for j in range(AHEAD):
        send(j)

    slot, expert = slots((EXPERTS, EXPERTS * CAP), 1)
    spread = jnp.where(expert == lax.broadcasted_iota(jnp.int32, expert.shape, 0), 1.0, 0.0).astype(BF16)
    turned = ((1,), (1,))
    chosen = dot(dot(eye, rank, turned).astype(BF16), spread) == slot
    for table, part in ((mixhi_ref, gate_hi), (mixlo_ref, gate_lo)):
        spread_gate = dot(dot(eye, part, turned).astype(BF16), spread)
        whole = jnp.where(chosen, spread_gate, 0.0).astype(BF16)
        for j in range(CHUNKS):
            table[j] = whole[:, j * ROWS : (j + 1) * ROWS]

    for copy in weights:
        copy.wait()
    for swap in swaps:
        swap.wait()

    for j in range(CHUNKS):
        if j + AHEAD < CHUNKS:
            each_peer(j, lambda i: send_copy(i).wait_send())
            send(j + AHEAD)
        if j == 0:
            own_out.wait()
        each_peer(j, lambda i: send_copy(i).wait_recv())
        tiles_in(in_rows, j)

        def hidden(n, carry):
            half, at = n // 2, pl.ds(pl.multiple_of((n % 2) * 256, 256), 256)
            gate = dot(x_ref[...], wg_ref[half, :, at])
            up = dot(x_ref[...], wu_ref[half, :, at])
            h_ref[:, pl.ds(pl.multiple_of(n * 256, 256), 256)] = (gate / (1.0 + jnp.exp(-gate)) * up).astype(BF16)
            return carry

        lax.fori_loop(0, 4, hidden, 0)

        def down(n, carry):
            at = pl.ds(pl.multiple_of(n * 256, 256), 256)
            rows = dot(h_ref[:, :HALF], wd_ref[0, :, at]) + dot(h_ref[:, HALF:], wd_ref[1, :, at])
            wide_ref[pl.ds(2 * n, ROWS, stride=PIECES), :] = rows[:, :LANES]
            wide_ref[pl.ds(2 * n + 1, ROWS, stride=PIECES), :] = rows[:, LANES:]
            return carry

        lax.fori_loop(0, D // 256, down, 0, unroll=2)
        tiles_out(done_rows, j)
        if j == 0:
            own_back.start()
        each_peer(j, lambda i: back_copy(i).start())

    for j in range(CHUNKS):
        if j == 0:
            own_back.wait()
        each_peer(j, lambda i: back_copy(i).wait_recv())
        tiles_in(back_rows, j)
        for n in range(D // 512):
            at = slice(n * 512, (n + 1) * 512)
            stream_ref[:, at] += dot(mixhi_ref[j], x_ref[:, at]) + dot(mixlo_ref[j], x_ref[:, at])
    out_ref[...] = stream_ref[...].astype(BF16)

    for j in range(CHUNKS):
        if j + AHEAD >= CHUNKS:
            each_peer(j, lambda i: send_copy(i).wait_send())
        each_peer(j, lambda i: back_copy(i).wait_send())


def append_kernel(
    length_hbm, kv_hbm, cache_hbm, out_hbm, keys_ref, values_ref, length_ref, held, new, flat_ref, in_sem, out_sem
):
    fetch = pltpu.make_async_copy(kv_hbm, new, in_sem.at[GROUPS + 1])
    place = pltpu.make_async_copy(length_hbm, length_ref, in_sem.at[GROUPS + 2])

    def moves(g):
        at = pl.ds(pl.multiple_of(g * WIDE, WIDE), WIDE)
        arrive = pltpu.make_async_copy(cache_hbm.at[:, :, at], held.at[:, :, at], in_sem.at[g])
        leave = pltpu.make_async_copy(held.at[:, :, at], out_hbm.at[:, :, at], out_sem.at[g])
        return arrive, leave

    place.start()
    fetch.start()
    for g in range(GROUPS):
        moves(g)[0].start()
    fetch.wait()
    place.wait()

    def group(g, carry):
        arrive, leave = moves(g)
        arrive.wait()
        leave.start()
        for k in range(HEADS // GROUPS):
            turn(g * (HEADS // GROUPS) + k, k)
        return carry

    def turn(h, k):
        at = pl.ds(pl.multiple_of(h * HEAD_DIM, HEAD_DIM), HEAD_DIM)
        flat = flat_ref.at[k]
        for p in range(0, SEEN, STEP):
            flat[2 * p : 2 * (p + STEP), :] = held[p : p + STEP, :, at].reshape(2 * STEP, HEAD_DIM).astype(F32)
        flat[2 * SEEN : PAIRS, :] = new[:, :, at].reshape(2 * GROUP, HEAD_DIM).astype(F32)
        keys_ref[h] = flat[pl.ds(0, SEEN + GROUP, stride=2), :].astype(BF16)
        values_ref[h] = flat[pl.ds(1, SEEN + GROUP, stride=2), :].astype(BF16)

    lax.fori_loop(0, GROUPS, group, 0)
    for g in range(GROUPS):
        moves(g)[1].wait()
    write = pltpu.make_async_copy(new, out_hbm.at[pl.ds(length_ref[0], GROUP)], out_sem.at[GROUPS])
    write.start()
    write.wait()


def shards(
    queries, new_kv, cache, lengths, residual, out_weight, norm_gain, expert_ids, gates, w_gate, w_up, w_down
):
    anywhere = pl.BlockSpec(memory_space=pl.ANY)
    in_vmem = pl.BlockSpec(memory_space=pltpu.VMEM)
    tiles = (EXPERTS, CAP, PIECES, LANES)
    appended, keys, values = pl.pallas_call(
        append_kernel,
        name="append",
        out_shape=(
            jax.ShapeDtypeStruct((CACHE, 2, D), BF16),
            pltpu.VMEM((HEADS, SEEN + GROUP, HEAD_DIM), BF16),
            pltpu.VMEM((HEADS, SEEN + GROUP, HEAD_DIM), BF16),
        ),
        in_specs=[anywhere, anywhere, anywhere],
        out_specs=(anywhere, in_vmem, in_vmem),
        scratch_shapes=[
            pltpu.SMEM((1,), jnp.int32),
            pltpu.VMEM((CACHE, 2, D), BF16),
            pltpu.VMEM((GROUP, 2, D), BF16),
            pltpu.VMEM((HEADS // GROUPS, PAIRS, HEAD_DIM), F32),
            pltpu.SemaphoreType.DMA((GROUPS + 3,)),
            pltpu.SemaphoreType.DMA((GROUPS + 1,)),
        ],
        compiler_params=pltpu.CompilerParams(vmem_limit_bytes=58 * 1024 * 1024),
    )(lengths, new_kv[0], cache[0])
    layer_out = pl.pallas_call(
        layer_kernel,
        name="layer",
        out_shape=pltpu.VMEM((GROUP, D), BF16),
        in_specs=[anywhere] * 5 + [in_vmem, in_vmem] + [anywhere] * 5,
        out_specs=in_vmem,
        scratch_shapes=[
            pltpu.SMEM((1,), jnp.int32),
            pltpu.VMEM((8, SEEN + GROUP), F32),
            pltpu.VMEM((TOP, GROUP), jnp.int32),
            pltpu.VMEM((TOP, GROUP), F32),
            pltpu.VMEM((1, D), F32),
            pltpu.VMEM((GROUP, D), BF16),
            pltpu.VMEM((GROUP, D), BF16),
            pltpu.VMEM((D, D), BF16),
            pltpu.VMEM((2, D, HALF), BF16),
            pltpu.VMEM((2, D, HALF), BF16),
            pltpu.VMEM((2, HALF, D), BF16),
            pltpu.VMEM((GROUP, D), BF16),
            pltpu.VMEM((GROUP, D), F32),
            pltpu.VMEM((GROUP, D), BF16),
            pltpu.VMEM((EXPERTS * CAP, GROUP), BF16),
            pltpu.VMEM((CHUNKS, GROUP, ROWS), BF16),
            pltpu.VMEM((CHUNKS, GROUP, ROWS), BF16),
            pltpu.VMEM((ROWS * PIECES, LANES), F32),
            pltpu.VMEM((ROWS, D), BF16),
            pltpu.VMEM((ROWS, 2 * HALF), BF16),
            pltpu.VMEM(tiles, BF16),
            pltpu.VMEM(tiles, BF16),
            pltpu.VMEM(tiles, BF16),
            pltpu.VMEM(tiles, BF16),
            pltpu.SemaphoreType.DMA((9,)),
            pltpu.SemaphoreType.DMA((GROUPS,)),
            pltpu.SemaphoreType.DMA((3,)),
            pltpu.SemaphoreType.DMA((3,)),
            pltpu.SemaphoreType.DMA((EXPERTS,)),
            pltpu.SemaphoreType.DMA((EXPERTS,)),
            pltpu.SemaphoreType.DMA((EXPERTS,)),
            pltpu.SemaphoreType.DMA((EXPERTS,)),
        ],
        compiler_params=pltpu.CompilerParams(
            collective_id=0, has_side_effects=True, vmem_limit_bytes=58 * 1024 * 1024
        ),
    )(
        lengths,
        expert_ids[0].T,
        gates[0].T,
        norm_gain[None],
        queries[0],
        pltpu.with_memory_space_constraint(keys, pltpu.VMEM),
        pltpu.with_memory_space_constraint(values, pltpu.VMEM),
        residual[0],
        out_weight,
        w_gate[0],
        w_up[0],
        w_down[0],
    )
    return layer_out[None], appended[None]


def solution(mesh):
    shared = ("req", "exp")
    three, four = P(shared, None, None), P(shared, None, None, None)
    return jax.shard_map(
        shards,
        mesh=mesh,
        in_specs=(three, four, four, P(shared), three, P(), P(), three, three, three, three, three),
        out_specs=(three, four),
        check_vma=False,
    )
```

```python
import math

import jax
import jax.numpy as jnp
from jax import lax
from jax.experimental import pallas as pl
from jax.experimental.pallas import tpu as pltpu
from jax.sharding import PartitionSpec as P

MESH = pl.DeviceIdType.MESH
F32 = jnp.float32
BF16 = jnp.bfloat16

GROUP = 64
D = 2048
HEADS = 16
HEAD_DIM = 128
EXPERTS = 64
TOP = 8
HALF = 512
CAP = 10
CACHE = 512
SEEN = 448
LANES = 128
PIECES = D // LANES
CHUNKS = 4
PEERS = EXPERTS // CHUNKS
ROWS = PEERS * CAP
MASKED = -1e30 * HEAD_DIM**0.5
AHEAD = 2
GROUPS = 4
STEP = 16
WIDE = D // GROUPS
PAIRS = 2 * (SEEN + GROUP)
SCALE = HEAD_DIM ** (-0.5) / math.log(2.0)


def dot(a, b, dims=((1,), (0,))):
    return lax.dot_general(a, b, (dims, ((), ())), preferred_element_type=F32)


def offsets(i):
    dx, dy = (i // 4) % 4, i % 4
    return (i // PEERS + 8 - dx - dy) % 4, dx, dy


def layer_kernel(
    length_hbm,
    ids_hbm,
    gates_hbm,
    gain_hbm,
    q_hbm,
    keys_ref,
    values_ref,
    res_hbm,
    ow_hbm,
    wg_hbm,
    wu_hbm,
    wd_hbm,
    out_ref,
    length_ref,
    keep_ref,
    ids_ref,
    gates_ref,
    gain_ref,
    q_ref,
    res_ref,
    ow_ref,
    wg_ref,
    wu_ref,
    wd_ref,
    att_ref,
    stream_ref,
    normed_ref,
    pick_ref,
    mixhi_ref,
    mixlo_ref,
    wide_ref,
    x_ref,
    h_ref,
    out_rows,
    in_rows,
    done_rows,
    back_rows,
    local_sem,
    ow_sem,
    mate_send,
    mate_recv,
    send_sem,
    recv_sem,
    back_send,
    back_recv,
):
    z = lax.axis_index("req")
    along = lax.axis_index("exp")
    core = along % 2
    x = along // 8
    y = (along // 2) % 4

    zs = [lax.rem(z + d, 4) for d in range(4)]
    xs = [lax.rem(x + d, 4) * 8 for d in range(4)]
    ys = [lax.rem(y + d, 4) * 2 + core for d in range(4)]

    def device(i, sign):
        dz, dx, dy = (sign * d % 4 for d in offsets(i))
        return {"req": zs[dz], "exp": xs[dx] + ys[dy]}

    mate = {"req": z, "exp": along + 1 - 2 * core}

    small = [
        pltpu.make_async_copy(q_hbm, q_ref, local_sem.at[0]),
        pltpu.make_async_copy(length_hbm, length_ref, local_sem.at[1]),
        pltpu.make_async_copy(res_hbm, res_ref, local_sem.at[2]),
        pltpu.make_async_copy(gain_hbm, gain_ref, local_sem.at[6]),
    ]
    tables = [
        pltpu.make_async_copy(ids_hbm, ids_ref, local_sem.at[7]),
        pltpu.make_async_copy(gates_hbm, gates_ref, local_sem.at[8]),
    ]
    weights = [
        pltpu.make_async_copy(wg_hbm, wg_ref.at[core], local_sem.at[3]),
        pltpu.make_async_copy(wu_hbm, wu_ref.at[core], local_sem.at[4]),
        pltpu.make_async_copy(wd_hbm, wd_ref.at[core], local_sem.at[5]),
    ]

    def ow_copy(g):
        at = pl.ds(pl.multiple_of(g * WIDE, WIDE), WIDE)
        return pltpu.make_async_copy(ow_hbm.at[at], ow_ref.at[at], ow_sem.at[g])

    for copy in tables + small:
        copy.start()

    for g in range(GROUPS):
        ow_copy(g).start()
    barrier = pltpu.get_barrier_semaphore()

    for i in range(1, EXPERTS):
        pl.semaphore_signal(barrier, inc=1, device_id=device(i, 1), device_id_type=MESH)
    pl.semaphore_signal(barrier, inc=1, device_id=mate, device_id_type=MESH)

    swaps = [
        pltpu.make_async_remote_copy(
            src_ref=src, dst_ref=dst.at[core], send_sem=mate_send.at[k], recv_sem=mate_recv.at[k],
            device_id=mate, device_id_type=MESH,
        )
        for k, (src, dst) in enumerate(((wg_hbm, wg_ref), (wu_hbm, wu_ref), (wd_hbm, wd_ref)))
    ]

    for copy in tables:
        copy.wait()

    expert_of = lax.broadcasted_iota(jnp.int32, (EXPERTS, GROUP), 0)
    hit = jnp.zeros((EXPERTS, GROUP), F32)
    gate_of = jnp.zeros((EXPERTS, GROUP), F32)
    for k in range(TOP):
        same = ids_ref[k : k + 1, :] == expert_of
        hit = jnp.where(same, 1.0, hit)
        gate_of = jnp.where(same, gates_ref[k : k + 1, :], gate_of)
    t_row = lax.broadcasted_iota(jnp.int32, (GROUP, GROUP), 0)
    t_col = lax.broadcasted_iota(jnp.int32, (GROUP, GROUP), 1)
    before = jnp.where(t_row < t_col, 1.0, 0.0).astype(BF16)
    eye = jnp.where(t_row == t_col, 1.0, 0.0).astype(BF16)
    rank = dot(hit.astype(BF16), before)
    rank = jnp.where(hit > 0.5, rank, 99.0).astype(BF16)
    gate_hi = gate_of.astype(BF16)
    gate_lo = (gate_of - gate_hi.astype(F32)).astype(BF16)

    def slots(shape, axis):
        row = lax.broadcasted_iota(jnp.int32, shape, axis)
        i = (row * 6554) >> 16
        dx, dy = (i >> 2) & 3, i & 3
        dz = ((i >> 4) + 8 - dx - dy) & 3
        expert = (((z + dz) & 3) << 4) + (((x + dx) & 3) << 2) + ((y + dy) & 3)
        return (row - i * CAP).astype(F32), expert

    slot, expert = slots((EXPERTS * CAP, EXPERTS), 0)
    spread = jnp.where(expert == lax.broadcasted_iota(jnp.int32, expert.shape, 1), 1.0, 0.0).astype(BF16)
    pick_ref[...] = jnp.where(dot(spread, rank) == slot, 1.0, 0.0).astype(BF16)
    for copy in small:
        copy.wait()
    place = lax.broadcasted_iota(jnp.int32, (8, SEEN + GROUP), 1)
    length = length_ref[0]
    keep_ref[...] = jnp.where((place < length) | (place >= SEEN), 1.0, 0.0)

    def head(h):
        at = pl.ds(pl.multiple_of(h * HEAD_DIM, HEAD_DIM), HEAD_DIM)
        scores = dot(q_ref[:, at], keys_ref[h], ((1,), (1,)))
        scores = jnp.where(keep_ref[0:1, :] > 0.5, scores, MASKED)
        raised = jnp.exp2((scores - jnp.max(scores, axis=1, keepdims=True)) * SCALE)
        total = jnp.sum(raised, axis=1, keepdims=True)
        att_ref[:, at] = (dot(raised.astype(BF16), values_ref[h]) / total).astype(BF16)

    def group(g, carry):
        heads = [g * (HEADS // GROUPS) + k for k in range(HEADS // GROUPS)]
        for h in heads:
            head(h)
        ow_copy(g).wait()
        at = pl.ds(pl.multiple_of(g * WIDE, WIDE), WIDE)
        for n in range(0, D, 512):
            stream_ref[:, n : n + 512] += dot(att_ref[:, at], ow_ref[at, n : n + 512])
        return carry

    stream_ref[...] = res_ref[...].astype(F32)
    lax.fori_loop(0, 1, group, 0)
    pl.semaphore_wait(barrier, EXPERTS)
    for swap in swaps:
        swap.start()
    lax.fori_loop(1, GROUPS, group, 0)
    for copy in weights:
        copy.start()

    stream = stream_ref[...]
    mean_square = jnp.mean(stream * stream, axis=1, keepdims=True)
    normed_ref[...] = (stream * lax.rsqrt(mean_square + 1e-06) * gain_ref[...]).astype(BF16)

    def send_copy(j, part, peer):
        return pltpu.make_async_remote_copy(
            src_ref=out_rows.at[part], dst_ref=in_rows.at[part], send_sem=send_sem.at[j], recv_sem=recv_sem.at[j],
            device_id=peer, device_id_type=MESH,
        )

    def back_copy(j, part, peer):
        return pltpu.make_async_remote_copy(
            src_ref=done_rows.at[part], dst_ref=back_rows.at[part], send_sem=back_send.at[j],
            recv_sem=back_recv.at[j], device_id=peer, device_id_type=MESH,
        )

    def start_chunk(copy, j, sign):
        for i in range(max(j * PEERS, 1), (j + 1) * PEERS):
            copy(j, pl.ds(i, 1), device(i, sign)).start()

    def chunk_sent(copy, j):
        first = max(j * PEERS, 1)
        copy(j, pl.ds(first, (j + 1) * PEERS - first), mate).wait_send()

    def chunk_here(copy, j):
        copy(j, pl.ds(j * PEERS, PEERS), mate).wait_recv()

    own_out = pltpu.make_async_copy(out_rows.at[pl.ds(0, 1)], in_rows.at[pl.ds(0, 1)], recv_sem.at[0])
    own_back = pltpu.make_async_copy(done_rows.at[pl.ds(0, 1)], back_rows.at[pl.ds(0, 1)], back_recv.at[0])

    def tiles_out(rows, j):
        rows[pl.ds(j * PEERS, PEERS)] = wide_ref[...].reshape(PEERS, CAP, PIECES, LANES).astype(BF16)

    def tiles_in(rows, j):
        wide_ref[...] = rows[pl.ds(j * PEERS, PEERS)].astype(F32).reshape(ROWS * PIECES, LANES)
        for c in range(PIECES):
            x_ref[:, c * LANES : (c + 1) * LANES] = wide_ref[pl.ds(c, ROWS, stride=PIECES), :].astype(BF16)

    def send(j):
        picked = pick_ref[j * ROWS : (j + 1) * ROWS, :]
        for c in range(PIECES):
            wide_ref[pl.ds(c, ROWS, stride=PIECES), :] = dot(picked, normed_ref[:, c * LANES : (c + 1) * LANES])
        tiles_out(out_rows, j)
        if j == 0:
            own_out.start()
        start_chunk(send_copy, j, 1)

    for j in range(AHEAD):
        send(j)

    slot, expert = slots((EXPERTS, EXPERTS * CAP), 1)
    spread = jnp.where(expert == lax.broadcasted_iota(jnp.int32, expert.shape, 0), 1.0, 0.0).astype(BF16)
    turned = ((1,), (1,))
    chosen = dot(dot(eye, rank, turned).astype(BF16), spread) == slot
    for table, part in ((mixhi_ref, gate_hi), (mixlo_ref, gate_lo)):
        spread_gate = dot(dot(eye, part, turned).astype(BF16), spread)
        whole = jnp.where(chosen, spread_gate, 0.0).astype(BF16)
        for j in range(CHUNKS):
            table[j] = whole[:, j * ROWS : (j + 1) * ROWS]

    for copy in weights:
        copy.wait()
    for swap in swaps:
        swap.wait()

    for j in range(CHUNKS):
        if j + AHEAD < CHUNKS:
            chunk_sent(send_copy, j)
            send(j + AHEAD)
        chunk_here(send_copy, j)
        tiles_in(in_rows, j)

        def hidden(n, carry):
            half, at = n // 2, pl.ds(pl.multiple_of((n % 2) * 256, 256), 256)
            gate = dot(x_ref[...], wg_ref[half, :, at])
            up = dot(x_ref[...], wu_ref[half, :, at])
            h_ref[:, pl.ds(pl.multiple_of(n * 256, 256), 256)] = (gate / (1.0 + jnp.exp(-gate)) * up).astype(BF16)
            return carry

        lax.fori_loop(0, 4, hidden, 0)

        def down(n, carry):
            at = pl.ds(pl.multiple_of(n * 256, 256), 256)
            rows = dot(h_ref[:, :HALF], wd_ref[0, :, at]) + dot(h_ref[:, HALF:], wd_ref[1, :, at])
            wide_ref[pl.ds(2 * n, ROWS, stride=PIECES), :] = rows[:, :LANES]
            wide_ref[pl.ds(2 * n + 1, ROWS, stride=PIECES), :] = rows[:, LANES:]
            return carry

        lax.fori_loop(0, D // 256, down, 0, unroll=2)
        tiles_out(done_rows, j)
        if j == 0:
            own_back.start()
        start_chunk(back_copy, j, -1)

    for j in range(CHUNKS):
        chunk_here(back_copy, j)
        tiles_in(back_rows, j)
        for n in range(D // 512):
            at = slice(n * 512, (n + 1) * 512)
            stream_ref[:, at] += dot(mixhi_ref[j], x_ref[:, at]) + dot(mixlo_ref[j], x_ref[:, at])
    out_ref[...] = stream_ref[...].astype(BF16)

    for j in range(CHUNKS):
        if j + AHEAD >= CHUNKS:
            chunk_sent(send_copy, j)
        chunk_sent(back_copy, j)


def append_kernel(
    length_hbm, kv_hbm, cache_hbm, out_hbm, keys_ref, values_ref, length_ref, held, new, flat_ref, in_sem, out_sem
):
    fetch = pltpu.make_async_copy(kv_hbm, new, in_sem.at[GROUPS + 1])
    place = pltpu.make_async_copy(length_hbm, length_ref, in_sem.at[GROUPS + 2])

    def moves(g):
        at = pl.ds(pl.multiple_of(g * WIDE, WIDE), WIDE)
        arrive = pltpu.make_async_copy(cache_hbm.at[:, :, at], held.at[:, :, at], in_sem.at[g])
        leave = pltpu.make_async_copy(held.at[:, :, at], out_hbm.at[:, :, at], out_sem.at[g])
        return arrive, leave

    place.start()
    fetch.start()
    for g in range(GROUPS):
        moves(g)[0].start()
    fetch.wait()
    place.wait()

    def group(g, carry):
        arrive, leave = moves(g)
        arrive.wait()
        leave.start()
        for k in range(HEADS // GROUPS):
            turn(g * (HEADS // GROUPS) + k, k)
        return carry

    def turn(h, k):
        at = pl.ds(pl.multiple_of(h * HEAD_DIM, HEAD_DIM), HEAD_DIM)
        flat = flat_ref.at[k]
        for p in range(0, SEEN, STEP):
            flat[2 * p : 2 * (p + STEP), :] = held[p : p + STEP, :, at].reshape(2 * STEP, HEAD_DIM).astype(F32)
        flat[2 * SEEN : PAIRS, :] = new[:, :, at].reshape(2 * GROUP, HEAD_DIM).astype(F32)
        keys_ref[h] = flat[pl.ds(0, SEEN + GROUP, stride=2), :].astype(BF16)
        values_ref[h] = flat[pl.ds(1, SEEN + GROUP, stride=2), :].astype(BF16)

    lax.fori_loop(0, GROUPS, group, 0)
    for g in range(GROUPS):
        moves(g)[1].wait()
    write = pltpu.make_async_copy(new, out_hbm.at[pl.ds(length_ref[0], GROUP)], out_sem.at[GROUPS])
    write.start()
    write.wait()


def shards(
    queries, new_kv, cache, lengths, residual, out_weight, norm_gain, expert_ids, gates, w_gate, w_up, w_down
):
    anywhere = pl.BlockSpec(memory_space=pl.ANY)
    in_vmem = pl.BlockSpec(memory_space=pltpu.VMEM)
    tiles = (EXPERTS, CAP, PIECES, LANES)
    appended, keys, values = pl.pallas_call(
        append_kernel,
        name="append",
        out_shape=(
            jax.ShapeDtypeStruct((CACHE, 2, D), BF16),
            pltpu.VMEM((HEADS, SEEN + GROUP, HEAD_DIM), BF16),
            pltpu.VMEM((HEADS, SEEN + GROUP, HEAD_DIM), BF16),
        ),
        in_specs=[anywhere, anywhere, anywhere],
        out_specs=(anywhere, in_vmem, in_vmem),
        scratch_shapes=[
            pltpu.SMEM((1,), jnp.int32),
            pltpu.VMEM((CACHE, 2, D), BF16),
            pltpu.VMEM((GROUP, 2, D), BF16),
            pltpu.VMEM((HEADS // GROUPS, PAIRS, HEAD_DIM), F32),
            pltpu.SemaphoreType.DMA((GROUPS + 3,)),
            pltpu.SemaphoreType.DMA((GROUPS + 1,)),
        ],
        compiler_params=pltpu.CompilerParams(vmem_limit_bytes=58 * 1024 * 1024),
    )(lengths, new_kv[0], cache[0])
    layer_out = pl.pallas_call(
        layer_kernel,
        name="layer",
        out_shape=pltpu.VMEM((GROUP, D), BF16),
        in_specs=[anywhere] * 5 + [in_vmem, in_vmem] + [anywhere] * 5,
        out_specs=in_vmem,
        scratch_shapes=[
            pltpu.SMEM((1,), jnp.int32),
            pltpu.VMEM((8, SEEN + GROUP), F32),
            pltpu.VMEM((TOP, GROUP), jnp.int32),
            pltpu.VMEM((TOP, GROUP), F32),
            pltpu.VMEM((1, D), F32),
            pltpu.VMEM((GROUP, D), BF16),
            pltpu.VMEM((GROUP, D), BF16),
            pltpu.VMEM((D, D), BF16),
            pltpu.VMEM((2, D, HALF), BF16),
            pltpu.VMEM((2, D, HALF), BF16),
            pltpu.VMEM((2, HALF, D), BF16),
            pltpu.VMEM((GROUP, D), BF16),
            pltpu.VMEM((GROUP, D), F32),
            pltpu.VMEM((GROUP, D), BF16),
            pltpu.VMEM((EXPERTS * CAP, GROUP), BF16),
            pltpu.VMEM((CHUNKS, GROUP, ROWS), BF16),
            pltpu.VMEM((CHUNKS, GROUP, ROWS), BF16),
            pltpu.VMEM((ROWS * PIECES, LANES), F32),
            pltpu.VMEM((ROWS, D), BF16),
            pltpu.VMEM((ROWS, 2 * HALF), BF16),
            pltpu.VMEM(tiles, BF16),
            pltpu.VMEM(tiles, BF16),
            pltpu.VMEM(tiles, BF16),
            pltpu.VMEM(tiles, BF16),
            pltpu.SemaphoreType.DMA((9,)),
            pltpu.SemaphoreType.DMA((GROUPS,)),
            pltpu.SemaphoreType.DMA((3,)),
            pltpu.SemaphoreType.DMA((3,)),
            pltpu.SemaphoreType.DMA((CHUNKS,)),
            pltpu.SemaphoreType.DMA((CHUNKS,)),
            pltpu.SemaphoreType.DMA((CHUNKS,)),
            pltpu.SemaphoreType.DMA((CHUNKS,)),
        ],
        compiler_params=pltpu.CompilerParams(
            collective_id=0, has_side_effects=True, vmem_limit_bytes=58 * 1024 * 1024
        ),
    )(
        lengths,
        expert_ids[0].T,
        gates[0].T,
        norm_gain[None],
        queries[0],
        pltpu.with_memory_space_constraint(keys, pltpu.VMEM),
        pltpu.with_memory_space_constraint(values, pltpu.VMEM),
        residual[0],
        out_weight,
        w_gate[0],
        w_up[0],
        w_down[0],
    )
    return layer_out[None], appended[None]


def solution(mesh):
    shared = ("req", "exp")
    three, four = P(shared, None, None), P(shared, None, None, None)
    return jax.shard_map(
        shards,
        mesh=mesh,
        in_specs=(three, four, four, P(shared), three, P(), P(), three, three, three, three, three),
        out_specs=(three, four),
        check_vma=False,
    )
```

```python
import math

import jax
import jax.numpy as jnp
from jax import lax
from jax.experimental import pallas as pl
from jax.experimental.pallas import tpu as pltpu
from jax.sharding import PartitionSpec as P

MESH = pl.DeviceIdType.MESH
F32 = jnp.float32
BF16 = jnp.bfloat16

GROUP = 64
D = 2048
HEADS = 16
HEAD_DIM = 128
EXPERTS = 64
TOP = 8
HALF = 512
CAP = 10
CACHE = 512
SEEN = 448
LANES = 128
PIECES = D // LANES
CHUNKS = 4
PEERS = EXPERTS // CHUNKS
ROWS = PEERS * CAP
MASKED = -1e30 * HEAD_DIM**0.5
AHEAD = 2
GROUPS = 4
STEP = 16
WIDE = D // GROUPS
PAIRS = 2 * (SEEN + GROUP)
SCALE = HEAD_DIM ** (-0.5) / math.log(2.0)


def dot(a, b, dims=((1,), (0,))):
    return lax.dot_general(a, b, (dims, ((), ())), preferred_element_type=F32)


def offsets(i):
    dx, dy = (i // 4) % 4, i % 4
    return (i // PEERS + 8 - dx - dy) % 4, dx, dy


def layer_kernel(
    length_hbm,
    ids_hbm,
    gates_hbm,
    gain_hbm,
    q_hbm,
    keys_ref,
    values_ref,
    res_hbm,
    ow_hbm,
    wg_hbm,
    wu_hbm,
    wd_hbm,
    out_ref,
    length_ref,
    keep_ref,
    ids_ref,
    gates_ref,
    gain_ref,
    q_ref,
    res_ref,
    ow_ref,
    wg_ref,
    wu_ref,
    wd_ref,
    att_ref,
    stream_ref,
    normed_ref,
    pick_ref,
    mixhi_ref,
    mixlo_ref,
    wide_ref,
    x_ref,
    h_ref,
    out_rows,
    in_rows,
    done_rows,
    back_rows,
    local_sem,
    ow_sem,
    mate_send,
    mate_recv,
    send_sem,
    recv_sem,
    back_send,
    back_recv,
):
    z = lax.axis_index("req")
    along = lax.axis_index("exp")
    core = along % 2
    x = along // 8
    y = (along // 2) % 4

    def device(i, sign):
        dz, dx, dy = offsets(i)
        there = (((x + sign * dx + 4) % 4) * 4 + (y + sign * dy + 4) % 4) * 2 + core
        return {"req": (z + sign * dz + 4) % 4, "exp": there}

    mate = {"req": z, "exp": along + 1 - 2 * core}

    small = [
        pltpu.make_async_copy(q_hbm, q_ref, local_sem.at[0]),
        pltpu.make_async_copy(length_hbm, length_ref, local_sem.at[1]),
        pltpu.make_async_copy(res_hbm, res_ref, local_sem.at[2]),
        pltpu.make_async_copy(gain_hbm, gain_ref, local_sem.at[6]),
    ]
    tables = [
        pltpu.make_async_copy(ids_hbm, ids_ref, local_sem.at[7]),
        pltpu.make_async_copy(gates_hbm, gates_ref, local_sem.at[8]),
    ]
    weights = [
        pltpu.make_async_copy(wg_hbm, wg_ref.at[core], local_sem.at[3]),
        pltpu.make_async_copy(wu_hbm, wu_ref.at[core], local_sem.at[4]),
        pltpu.make_async_copy(wd_hbm, wd_ref.at[core], local_sem.at[5]),
    ]

    def ow_copy(g):
        at = pl.ds(pl.multiple_of(g * WIDE, WIDE), WIDE)
        return pltpu.make_async_copy(ow_hbm.at[at], ow_ref.at[at], ow_sem.at[g])

    for copy in tables + small:
        copy.start()

    for g in range(GROUPS):
        ow_copy(g).start()
    barrier = pltpu.get_barrier_semaphore()

    def greet(i, carry):
        pl.semaphore_signal(barrier, inc=1, device_id=device(i, 1), device_id_type=MESH)
        return carry

    lax.fori_loop(1, EXPERTS, greet, 0)
    pl.semaphore_signal(barrier, inc=1, device_id=mate, device_id_type=MESH)

    swaps = [
        pltpu.make_async_remote_copy(
            src_ref=src, dst_ref=dst.at[core], send_sem=mate_send.at[k], recv_sem=mate_recv.at[k],
            device_id=mate, device_id_type=MESH,
        )
        for k, (src, dst) in enumerate(((wg_hbm, wg_ref), (wu_hbm, wu_ref), (wd_hbm, wd_ref)))
    ]

    for copy in tables:
        copy.wait()

    expert_of = lax.broadcasted_iota(jnp.int32, (EXPERTS, GROUP), 0)
    hit = jnp.zeros((EXPERTS, GROUP), F32)
    gate_of = jnp.zeros((EXPERTS, GROUP), F32)
    for k in range(TOP):
        same = ids_ref[k : k + 1, :] == expert_of
        hit = jnp.where(same, 1.0, hit)
        gate_of = jnp.where(same, gates_ref[k : k + 1, :], gate_of)
    t_row = lax.broadcasted_iota(jnp.int32, (GROUP, GROUP), 0)
    t_col = lax.broadcasted_iota(jnp.int32, (GROUP, GROUP), 1)
    before = jnp.where(t_row < t_col, 1.0, 0.0).astype(BF16)
    eye = jnp.where(t_row == t_col, 1.0, 0.0).astype(BF16)
    rank = dot(hit.astype(BF16), before)
    rank = jnp.where(hit > 0.5, rank, 99.0).astype(BF16)
    gate_hi = gate_of.astype(BF16)
    gate_lo = (gate_of - gate_hi.astype(F32)).astype(BF16)

    def slots(shape, axis):
        row = lax.broadcasted_iota(jnp.int32, shape, axis)
        i = (row * 6554) >> 16
        dx, dy = (i >> 2) & 3, i & 3
        dz = ((i >> 4) + 8 - dx - dy) & 3
        expert = (((z + dz) & 3) << 4) + (((x + dx) & 3) << 2) + ((y + dy) & 3)
        return (row - i * CAP).astype(F32), expert

    slot, expert = slots((EXPERTS * CAP, EXPERTS), 0)
    spread = jnp.where(expert == lax.broadcasted_iota(jnp.int32, expert.shape, 1), 1.0, 0.0).astype(BF16)
    pick_ref[...] = jnp.where(dot(spread, rank) == slot, 1.0, 0.0).astype(BF16)
    for copy in small:
        copy.wait()
    place = lax.broadcasted_iota(jnp.int32, (8, SEEN + GROUP), 1)
    length = length_ref[0]
    keep_ref[...] = jnp.where((place < length) | (place >= SEEN), 1.0, 0.0)

    def head(h):
        at = pl.ds(pl.multiple_of(h * HEAD_DIM, HEAD_DIM), HEAD_DIM)
        scores = dot(q_ref[:, at], keys_ref[h], ((1,), (1,)))
        scores = jnp.where(keep_ref[0:1, :] > 0.5, scores, MASKED)
        raised = jnp.exp2((scores - jnp.max(scores, axis=1, keepdims=True)) * SCALE)
        total = jnp.sum(raised, axis=1, keepdims=True)
        att_ref[:, at] = (dot(raised.astype(BF16), values_ref[h]) / total).astype(BF16)

    def group(g, carry):
        heads = [g * (HEADS // GROUPS) + k for k in range(HEADS // GROUPS)]
        for h in heads:
            head(h)
        ow_copy(g).wait()
        at = pl.ds(pl.multiple_of(g * WIDE, WIDE), WIDE)
        for n in range(0, D, 512):
            stream_ref[:, n : n + 512] += dot(att_ref[:, at], ow_ref[at, n : n + 512])
        return carry

    stream_ref[...] = res_ref[...].astype(F32)
    lax.fori_loop(0, 1, group, 0)
    pl.semaphore_wait(barrier, EXPERTS)
    for swap in swaps:
        swap.start()
    lax.fori_loop(1, GROUPS, group, 0)
    for copy in weights:
        copy.start()

    stream = stream_ref[...]
    mean_square = jnp.mean(stream * stream, axis=1, keepdims=True)
    normed_ref[...] = (stream * lax.rsqrt(mean_square + 1e-06) * gain_ref[...]).astype(BF16)

    def send_copy(i, peer=None):
        return pltpu.make_async_remote_copy(
            src_ref=out_rows.at[i], dst_ref=in_rows.at[i], send_sem=send_sem.at[i], recv_sem=recv_sem.at[i],
            device_id=peer or device(i, 1), device_id_type=MESH,
        )

    def back_copy(i, peer=None):
        return pltpu.make_async_remote_copy(
            src_ref=done_rows.at[i], dst_ref=back_rows.at[i], send_sem=back_send.at[i], recv_sem=back_recv.at[i],
            device_id=peer or device(i, -1), device_id_type=MESH,
        )

    own_out = pltpu.make_async_copy(out_rows.at[0], in_rows.at[0], recv_sem.at[0])
    own_back = pltpu.make_async_copy(done_rows.at[0], back_rows.at[0], back_recv.at[0])

    def tiles_out(rows, j):
        rows[pl.ds(j * PEERS, PEERS)] = wide_ref[...].reshape(PEERS, CAP, PIECES, LANES).astype(BF16)

    def tiles_in(rows, j):
        wide_ref[...] = rows[pl.ds(j * PEERS, PEERS)].astype(F32).reshape(ROWS * PIECES, LANES)
        for c in range(PIECES):
            x_ref[:, c * LANES : (c + 1) * LANES] = wide_ref[pl.ds(c, ROWS, stride=PIECES), :].astype(BF16)

    def each_peer(j, action):
        def body(i, carry):
            action(i)
            return carry

        lax.fori_loop(j * PEERS + (1 if j == 0 else 0), (j + 1) * PEERS, body, 0)

    def send(j):
        picked = pick_ref[j * ROWS : (j + 1) * ROWS, :]
        for c in range(PIECES):
            wide_ref[pl.ds(c, ROWS, stride=PIECES), :] = dot(picked, normed_ref[:, c * LANES : (c + 1) * LANES])
        tiles_out(out_rows, j)
        if j == 0:
            own_out.start()
        each_peer(j, lambda i: send_copy(i).start())

    for j in range(AHEAD):
        send(j)

    slot, expert = slots((EXPERTS, EXPERTS * CAP), 1)
    spread = jnp.where(expert == lax.broadcasted_iota(jnp.int32, expert.shape, 0), 1.0, 0.0).astype(BF16)
    turned = ((1,), (1,))
    chosen = dot(dot(eye, rank, turned).astype(BF16), spread) == slot
    for table, part in ((mixhi_ref, gate_hi), (mixlo_ref, gate_lo)):
        spread_gate = dot(dot(eye, part, turned).astype(BF16), spread)
        whole = jnp.where(chosen, spread_gate, 0.0).astype(BF16)
        for j in range(CHUNKS):
            table[j] = whole[:, j * ROWS : (j + 1) * ROWS]

    for copy in weights:
        copy.wait()
    for swap in swaps:
        swap.wait()

    for j in range(CHUNKS):
        if j + AHEAD < CHUNKS:
            each_peer(j, lambda i: send_copy(i).wait_send())
            send(j + AHEAD)
        if j == 0:
            own_out.wait()
        each_peer(j, lambda i: send_copy(i).wait_recv())
        tiles_in(in_rows, j)

        def hidden(n, carry):
            half, at = n // 2, pl.ds(pl.multiple_of((n % 2) * 256, 256), 256)
            gate = dot(x_ref[...], wg_ref[half, :, at])
            up = dot(x_ref[...], wu_ref[half, :, at])
            h_ref[:, pl.ds(pl.multiple_of(n * 256, 256), 256)] = (gate / (1.0 + jnp.exp(-gate)) * up).astype(BF16)
            return carry

        lax.fori_loop(0, 4, hidden, 0)

        def down(n, carry):
            at = pl.ds(pl.multiple_of(n * 256, 256), 256)
            rows = dot(h_ref[:, :HALF], wd_ref[0, :, at]) + dot(h_ref[:, HALF:], wd_ref[1, :, at])
            wide_ref[pl.ds(2 * n, ROWS, stride=PIECES), :] = rows[:, :LANES]
            wide_ref[pl.ds(2 * n + 1, ROWS, stride=PIECES), :] = rows[:, LANES:]
            return carry

        lax.fori_loop(0, D // 256, down, 0, unroll=2)
        tiles_out(done_rows, j)
        if j == 0:
            own_back.start()
        each_peer(j, lambda i: back_copy(i).start())

    for j in range(CHUNKS):
        if j == 0:
            own_back.wait()
        each_peer(j, lambda i: back_copy(i).wait_recv())
        tiles_in(back_rows, j)
        for n in range(D // 512):
            at = slice(n * 512, (n + 1) * 512)
            stream_ref[:, at] += dot(mixhi_ref[j], x_ref[:, at]) + dot(mixlo_ref[j], x_ref[:, at])
    out_ref[...] = stream_ref[...].astype(BF16)

    for i in range((CHUNKS - AHEAD) * PEERS, EXPERTS):
        send_copy(i, mate).wait_send()
    for i in range(1, EXPERTS):
        back_copy(i, mate).wait_send()


def append_kernel(
    length_hbm, kv_hbm, cache_hbm, out_hbm, keys_ref, values_ref, length_ref, held, new, flat_ref, in_sem, out_sem
):
    fetch = pltpu.make_async_copy(kv_hbm, new, in_sem.at[GROUPS + 1])
    place = pltpu.make_async_copy(length_hbm, length_ref, in_sem.at[GROUPS + 2])

    def moves(g):
        at = pl.ds(pl.multiple_of(g * WIDE, WIDE), WIDE)
        arrive = pltpu.make_async_copy(cache_hbm.at[:, :, at], held.at[:, :, at], in_sem.at[g])
        leave = pltpu.make_async_copy(held.at[:, :, at], out_hbm.at[:, :, at], out_sem.at[g])
        return arrive, leave

    place.start()
    fetch.start()
    for g in range(GROUPS):
        moves(g)[0].start()
    fetch.wait()
    place.wait()

    def group(g, carry):
        arrive, leave = moves(g)
        arrive.wait()
        leave.start()
        for k in range(HEADS // GROUPS):
            turn(g * (HEADS // GROUPS) + k, k)
        return carry

    def turn(h, k):
        at = pl.ds(pl.multiple_of(h * HEAD_DIM, HEAD_DIM), HEAD_DIM)
        flat = flat_ref.at[k]
        for p in range(0, SEEN, STEP):
            flat[2 * p : 2 * (p + STEP), :] = held[p : p + STEP, :, at].reshape(2 * STEP, HEAD_DIM).astype(F32)
        flat[2 * SEEN : PAIRS, :] = new[:, :, at].reshape(2 * GROUP, HEAD_DIM).astype(F32)
        keys_ref[h] = flat[pl.ds(0, SEEN + GROUP, stride=2), :].astype(BF16)
        values_ref[h] = flat[pl.ds(1, SEEN + GROUP, stride=2), :].astype(BF16)

    lax.fori_loop(0, GROUPS, group, 0)
    for g in range(GROUPS):
        moves(g)[1].wait()
    write = pltpu.make_async_copy(new, out_hbm.at[pl.ds(length_ref[0], GROUP)], out_sem.at[GROUPS])
    write.start()
    write.wait()


def shards(
    queries, new_kv, cache, lengths, residual, out_weight, norm_gain, expert_ids, gates, w_gate, w_up, w_down
):
    anywhere = pl.BlockSpec(memory_space=pl.ANY)
    in_vmem = pl.BlockSpec(memory_space=pltpu.VMEM)
    tiles = (EXPERTS, CAP, PIECES, LANES)
    appended, keys, values = pl.pallas_call(
        append_kernel,
        name="append",
        out_shape=(
            jax.ShapeDtypeStruct((CACHE, 2, D), BF16),
            pltpu.VMEM((HEADS, SEEN + GROUP, HEAD_DIM), BF16),
            pltpu.VMEM((HEADS, SEEN + GROUP, HEAD_DIM), BF16),
        ),
        in_specs=[anywhere, anywhere, anywhere],
        out_specs=(anywhere, in_vmem, in_vmem),
        scratch_shapes=[
            pltpu.SMEM((1,), jnp.int32),
            pltpu.VMEM((CACHE, 2, D), BF16),
            pltpu.VMEM((GROUP, 2, D), BF16),
            pltpu.VMEM((HEADS // GROUPS, PAIRS, HEAD_DIM), F32),
            pltpu.SemaphoreType.DMA((GROUPS + 3,)),
            pltpu.SemaphoreType.DMA((GROUPS + 1,)),
        ],
        compiler_params=pltpu.CompilerParams(vmem_limit_bytes=58 * 1024 * 1024),
    )(lengths, new_kv[0], cache[0])
    layer_out = pl.pallas_call(
        layer_kernel,
        name="layer",
        out_shape=pltpu.VMEM((GROUP, D), BF16),
        in_specs=[anywhere] * 5 + [in_vmem, in_vmem] + [anywhere] * 5,
        out_specs=in_vmem,
        scratch_shapes=[
            pltpu.SMEM((1,), jnp.int32),
            pltpu.VMEM((8, SEEN + GROUP), F32),
            pltpu.VMEM((TOP, GROUP), jnp.int32),
            pltpu.VMEM((TOP, GROUP), F32),
            pltpu.VMEM((1, D), F32),
            pltpu.VMEM((GROUP, D), BF16),
            pltpu.VMEM((GROUP, D), BF16),
            pltpu.VMEM((D, D), BF16),
            pltpu.VMEM((2, D, HALF), BF16),
            pltpu.VMEM((2, D, HALF), BF16),
            pltpu.VMEM((2, HALF, D), BF16),
            pltpu.VMEM((GROUP, D), BF16),
            pltpu.VMEM((GROUP, D), F32),
            pltpu.VMEM((GROUP, D), BF16),
            pltpu.VMEM((EXPERTS * CAP, GROUP), BF16),
            pltpu.VMEM((CHUNKS, GROUP, ROWS), BF16),
            pltpu.VMEM((CHUNKS, GROUP, ROWS), BF16),
            pltpu.VMEM((ROWS * PIECES, LANES), F32),
            pltpu.VMEM((ROWS, D), BF16),
            pltpu.VMEM((ROWS, 2 * HALF), BF16),
            pltpu.VMEM(tiles, BF16),
            pltpu.VMEM(tiles, BF16),
            pltpu.VMEM(tiles, BF16),
            pltpu.VMEM(tiles, BF16),
            pltpu.SemaphoreType.DMA((9,)),
            pltpu.SemaphoreType.DMA((GROUPS,)),
            pltpu.SemaphoreType.DMA((3,)),
            pltpu.SemaphoreType.DMA((3,)),
            pltpu.SemaphoreType.DMA((EXPERTS,)),
            pltpu.SemaphoreType.DMA((EXPERTS,)),
            pltpu.SemaphoreType.DMA((EXPERTS,)),
            pltpu.SemaphoreType.DMA((EXPERTS,)),
        ],
        compiler_params=pltpu.CompilerParams(
            collective_id=0, has_side_effects=True, vmem_limit_bytes=58 * 1024 * 1024
        ),
    )(
        lengths,
        expert_ids[0].T,
        gates[0].T,
        norm_gain[None],
        queries[0],
        pltpu.with_memory_space_constraint(keys, pltpu.VMEM),
        pltpu.with_memory_space_constraint(values, pltpu.VMEM),
        residual[0],
        out_weight,
        w_gate[0],
        w_up[0],
        w_down[0],
    )
    return layer_out[None], appended[None]


def solution(mesh):
    shared = ("req", "exp")
    three, four = P(shared, None, None), P(shared, None, None, None)
    return jax.shard_map(
        shards,
        mesh=mesh,
        in_specs=(three, four, four, P(shared), three, P(), P(), three, three, three, three, three),
        out_specs=(three, four),
        check_vma=False,
    )
```

```python
import math

import jax
import jax.numpy as jnp
from jax import lax
from jax.experimental import pallas as pl
from jax.experimental.pallas import tpu as pltpu
from jax.sharding import PartitionSpec as P

MESH = pl.DeviceIdType.MESH
F32 = jnp.float32
BF16 = jnp.bfloat16

GROUP = 64
D = 2048
HEADS = 16
HEAD_DIM = 128
EXPERTS = 64
TOP = 8
HALF = 512
CAP = 10
CACHE = 512
SEEN = 448
LANES = 128
PIECES = D // LANES
CHUNKS = 4
PEERS = EXPERTS // CHUNKS
BATCH = 8
ROWS = PEERS * CAP
MASKED = -1e30 * HEAD_DIM**0.5
AHEAD = 2
GROUPS = 4
STEP = 16
WIDE = D // GROUPS
PAIRS = 2 * (SEEN + GROUP)
SCALE = HEAD_DIM ** (-0.5) / math.log(2.0)


def dot(a, b, dims=((1,), (0,))):
    return lax.dot_general(a, b, (dims, ((), ())), preferred_element_type=F32)


def offsets(i):
    dx, dy = (i // 4) % 4, i % 4
    return (i // PEERS + 8 - dx - dy) % 4, dx, dy


def layer_kernel(
    length_hbm,
    ids_hbm,
    gates_hbm,
    gain_hbm,
    q_hbm,
    keys_ref,
    values_ref,
    res_hbm,
    ow_hbm,
    wg_hbm,
    wu_hbm,
    wd_hbm,
    out_ref,
    length_ref,
    keep_ref,
    ids_ref,
    gates_ref,
    gain_ref,
    q_ref,
    res_ref,
    ow_ref,
    wg_ref,
    wu_ref,
    wd_ref,
    att_ref,
    stream_ref,
    normed_ref,
    pick_ref,
    mixhi_ref,
    mixlo_ref,
    wide_ref,
    wide_even,
    wide_odd,
    x_ref,
    h_ref,
    out_rows,
    in_rows,
    done_rows,
    back_rows,
    local_sem,
    ow_sem,
    mate_send,
    mate_recv,
    send_sem,
    recv_sem,
    back_send,
    back_recv,
):
    z = lax.axis_index("req")
    along = lax.axis_index("exp")
    core = along % 2
    x = along // 8
    y = (along // 2) % 4

    def device(i, sign):
        dz, dx, dy = offsets(i)
        there = (((x + sign * dx + 4) % 4) * 4 + (y + sign * dy + 4) % 4) * 2 + core
        return {"req": (z + sign * dz + 4) % 4, "exp": there}

    mate = {"req": z, "exp": along + 1 - 2 * core}

    small = [
        pltpu.make_async_copy(q_hbm, q_ref, local_sem.at[0]),
        pltpu.make_async_copy(length_hbm, length_ref, local_sem.at[1]),
        pltpu.make_async_copy(res_hbm, res_ref, local_sem.at[2]),
        pltpu.make_async_copy(gain_hbm, gain_ref, local_sem.at[6]),
    ]
    tables = [
        pltpu.make_async_copy(ids_hbm, ids_ref, local_sem.at[7]),
        pltpu.make_async_copy(gates_hbm, gates_ref, local_sem.at[8]),
    ]
    weights = [
        pltpu.make_async_copy(wg_hbm, wg_ref.at[core], local_sem.at[3]),
        pltpu.make_async_copy(wu_hbm, wu_ref.at[core], local_sem.at[4]),
        pltpu.make_async_copy(wd_hbm, wd_ref.at[core], local_sem.at[5]),
    ]

    def ow_copy(g):
        at = pl.ds(pl.multiple_of(g * WIDE, WIDE), WIDE)
        return pltpu.make_async_copy(ow_hbm.at[at], ow_ref.at[at], ow_sem.at[g])

    for copy in tables + small:
        copy.start()

    for g in range(GROUPS):
        ow_copy(g).start()
    barrier = pltpu.get_barrier_semaphore()

    def greet(i, carry):
        pl.semaphore_signal(barrier, inc=1, device_id=device(i, 1), device_id_type=MESH)
        return carry

    lax.fori_loop(1, EXPERTS, greet, 0)
    pl.semaphore_signal(barrier, inc=1, device_id=mate, device_id_type=MESH)

    swaps = [
        pltpu.make_async_remote_copy(
            src_ref=src, dst_ref=dst.at[core], send_sem=mate_send.at[k], recv_sem=mate_recv.at[k],
            device_id=mate, device_id_type=MESH,
        )
        for k, (src, dst) in enumerate(((wg_hbm, wg_ref), (wu_hbm, wu_ref), (wd_hbm, wd_ref)))
    ]

    for copy in tables:
        copy.wait()

    expert_of = lax.broadcasted_iota(jnp.int32, (EXPERTS, GROUP), 0)
    hit = jnp.zeros((EXPERTS, GROUP), F32)
    gate_of = jnp.zeros((EXPERTS, GROUP), F32)
    for k in range(TOP):
        same = ids_ref[k : k + 1, :] == expert_of
        hit = jnp.where(same, 1.0, hit)
        gate_of = jnp.where(same, gates_ref[k : k + 1, :], gate_of)
    t_row = lax.broadcasted_iota(jnp.int32, (GROUP, GROUP), 0)
    t_col = lax.broadcasted_iota(jnp.int32, (GROUP, GROUP), 1)
    before = jnp.where(t_row < t_col, 1.0, 0.0).astype(BF16)
    eye = jnp.where(t_row == t_col, 1.0, 0.0).astype(BF16)
    rank = dot(hit.astype(BF16), before)
    rank = jnp.where(hit > 0.5, rank, 99.0).astype(BF16)
    gate_hi = gate_of.astype(BF16)
    gate_lo = (gate_of - gate_hi.astype(F32)).astype(BF16)

    def slots(shape, axis):
        row = lax.broadcasted_iota(jnp.int32, shape, axis)
        i = (row * 6554) >> 16
        dx, dy = (i >> 2) & 3, i & 3
        dz = ((i >> 4) + 8 - dx - dy) & 3
        expert = (((z + dz) & 3) << 4) + (((x + dx) & 3) << 2) + ((y + dy) & 3)
        return (row - i * CAP).astype(F32), expert

    slot, expert = slots((EXPERTS * CAP, EXPERTS), 0)
    spread = jnp.where(expert == lax.broadcasted_iota(jnp.int32, expert.shape, 1), 1.0, 0.0).astype(BF16)
    pick_ref[...] = jnp.where(dot(spread, rank) == slot, 1.0, 0.0).astype(BF16)
    for copy in small:
        copy.wait()
    place = lax.broadcasted_iota(jnp.int32, (8, SEEN + GROUP), 1)
    length = length_ref[0]
    keep_ref[...] = jnp.where((place < length) | (place >= SEEN), 1.0, 0.0)

    def head(h):
        at = pl.ds(pl.multiple_of(h * HEAD_DIM, HEAD_DIM), HEAD_DIM)
        scores = dot(q_ref[:, at], keys_ref[h], ((1,), (1,)))
        scores = jnp.where(keep_ref[0:1, :] > 0.5, scores, MASKED)
        raised = jnp.exp2((scores - jnp.max(scores, axis=1, keepdims=True)) * SCALE)
        total = jnp.sum(raised, axis=1, keepdims=True)
        att_ref[:, at] = (dot(raised.astype(BF16), values_ref[h]) / total).astype(BF16)

    def group(g, carry):
        heads = [g * (HEADS // GROUPS) + k for k in range(HEADS // GROUPS)]
        for h in heads:
            head(h)
        ow_copy(g).wait()
        at = pl.ds(pl.multiple_of(g * WIDE, WIDE), WIDE)
        for n in range(0, D, 512):
            stream_ref[:, n : n + 512] += dot(att_ref[:, at], ow_ref[at, n : n + 512])
        return carry

    stream_ref[...] = res_ref[...].astype(F32)
    lax.fori_loop(0, 1, group, 0)
    pl.semaphore_wait(barrier, EXPERTS)
    for swap in swaps:
        swap.start()
    lax.fori_loop(1, GROUPS, group, 0)
    for copy in weights:
        copy.start()

    stream = stream_ref[...]
    mean_square = jnp.mean(stream * stream, axis=1, keepdims=True)
    normed_ref[...] = (stream * lax.rsqrt(mean_square + 1e-06) * gain_ref[...]).astype(BF16)

    def send_copy(i, peer=None):
        return pltpu.make_async_remote_copy(
            src_ref=out_rows.at[i], dst_ref=in_rows.at[i], send_sem=send_sem.at[i], recv_sem=recv_sem.at[i],
            device_id=peer or device(i, 1), device_id_type=MESH,
        )

    def back_copy(i, peer=None):
        return pltpu.make_async_remote_copy(
            src_ref=done_rows.at[i], dst_ref=back_rows.at[i], send_sem=back_send.at[i], recv_sem=back_recv.at[i],
            device_id=peer or device(i, -1), device_id_type=MESH,
        )

    own_out = pltpu.make_async_copy(out_rows.at[0], in_rows.at[0], recv_sem.at[0])
    own_back = pltpu.make_async_copy(done_rows.at[0], back_rows.at[0], back_recv.at[0])

    wide_refs = (wide_even, wide_odd)

    def tiles_out(rows, j):
        rows[pl.ds(j * PEERS, PEERS)] = wide_ref[...].reshape(PEERS, CAP, PIECES, LANES).astype(BF16)

    def tiles_in(rows, j):
        for k in range(0, PEERS, BATCH):
            wide = wide_refs[k // BATCH % 2]
            size = BATCH * CAP
            wide[...] = rows[pl.ds(j * PEERS + k, BATCH)].astype(F32).reshape(size * PIECES, LANES)
            for c in range(PIECES):
                x_ref[k * CAP : k * CAP + size, c * LANES : (c + 1) * LANES] = wide[
                    pl.ds(c, size, stride=PIECES), :
                ].astype(BF16)

    def each_peer(j, action):
        def body(i, carry):
            action(i)
            return carry

        lax.fori_loop(j * PEERS + (1 if j == 0 else 0), (j + 1) * PEERS, body, 0)

    def send(j):
        picked = pick_ref[j * ROWS : (j + 1) * ROWS, :]
        for c in range(PIECES):
            wide_ref[pl.ds(c, ROWS, stride=PIECES), :] = dot(picked, normed_ref[:, c * LANES : (c + 1) * LANES])
        tiles_out(out_rows, j)
        if j == 0:
            own_out.start()
        each_peer(j, lambda i: send_copy(i).start())

    for j in range(AHEAD):
        send(j)

    slot, expert = slots((EXPERTS, EXPERTS * CAP), 1)
    spread = jnp.where(expert == lax.broadcasted_iota(jnp.int32, expert.shape, 0), 1.0, 0.0).astype(BF16)
    turned = ((1,), (1,))
    chosen = dot(dot(eye, rank, turned).astype(BF16), spread) == slot
    for table, part in ((mixhi_ref, gate_hi), (mixlo_ref, gate_lo)):
        spread_gate = dot(dot(eye, part, turned).astype(BF16), spread)
        whole = jnp.where(chosen, spread_gate, 0.0).astype(BF16)
        for j in range(CHUNKS):
            table[j] = whole[:, j * ROWS : (j + 1) * ROWS]

    for copy in weights:
        copy.wait()
    for swap in swaps:
        swap.wait()

    for j in range(CHUNKS):
        if j + AHEAD < CHUNKS:
            each_peer(j, lambda i: send_copy(i).wait_send())
            send(j + AHEAD)
        if j == 0:
            own_out.wait()
        each_peer(j, lambda i: send_copy(i).wait_recv())
        tiles_in(in_rows, j)

        def hidden(n, carry):
            half, at = n // 2, pl.ds(pl.multiple_of((n % 2) * 256, 256), 256)
            gate = dot(x_ref[...], wg_ref[half, :, at])
            up = dot(x_ref[...], wu_ref[half, :, at])
            h_ref[:, pl.ds(pl.multiple_of(n * 256, 256), 256)] = (gate / (1.0 + jnp.exp(-gate)) * up).astype(BF16)
            return carry

        lax.fori_loop(0, 4, hidden, 0)

        def down(n, carry):
            at = pl.ds(pl.multiple_of(n * 256, 256), 256)
            rows = dot(h_ref[:, :HALF], wd_ref[0, :, at]) + dot(h_ref[:, HALF:], wd_ref[1, :, at])
            wide_ref[pl.ds(2 * n, ROWS, stride=PIECES), :] = rows[:, :LANES]
            wide_ref[pl.ds(2 * n + 1, ROWS, stride=PIECES), :] = rows[:, LANES:]
            return carry

        lax.fori_loop(0, D // 256, down, 0, unroll=2)
        tiles_out(done_rows, j)
        if j == 0:
            own_back.start()
        each_peer(j, lambda i: back_copy(i).start())

    for j in range(CHUNKS):
        if j == 0:
            own_back.wait()
        each_peer(j, lambda i: back_copy(i).wait_recv())
        tiles_in(back_rows, j)
        for n in range(D // 512):
            at = slice(n * 512, (n + 1) * 512)
            stream_ref[:, at] += dot(mixhi_ref[j], x_ref[:, at]) + dot(mixlo_ref[j], x_ref[:, at])
    out_ref[...] = stream_ref[...].astype(BF16)

    for i in range((CHUNKS - AHEAD) * PEERS, EXPERTS):
        send_copy(i, mate).wait_send()
    for i in range(1, EXPERTS):
        back_copy(i, mate).wait_send()


def append_kernel(
    length_hbm, kv_hbm, cache_hbm, out_hbm, keys_ref, values_ref, length_ref, held, new, flat_ref, in_sem, out_sem
):
    fetch = pltpu.make_async_copy(kv_hbm, new, in_sem.at[GROUPS + 1])
    place = pltpu.make_async_copy(length_hbm, length_ref, in_sem.at[GROUPS + 2])

    def moves(g):
        at = pl.ds(pl.multiple_of(g * WIDE, WIDE), WIDE)
        arrive = pltpu.make_async_copy(cache_hbm.at[:, :, at], held.at[:, :, at], in_sem.at[g])
        leave = pltpu.make_async_copy(held.at[:, :, at], out_hbm.at[:, :, at], out_sem.at[g])
        return arrive, leave

    place.start()
    fetch.start()
    for g in range(GROUPS):
        moves(g)[0].start()
    fetch.wait()
    place.wait()

    def group(g, carry):
        arrive, leave = moves(g)
        arrive.wait()
        leave.start()
        for k in range(HEADS // GROUPS):
            turn(g * (HEADS // GROUPS) + k, k)
        return carry

    def turn(h, k):
        at = pl.ds(pl.multiple_of(h * HEAD_DIM, HEAD_DIM), HEAD_DIM)
        flat = flat_ref.at[k]
        for p in range(0, SEEN, STEP):
            flat[2 * p : 2 * (p + STEP), :] = held[p : p + STEP, :, at].reshape(2 * STEP, HEAD_DIM).astype(F32)
        flat[2 * SEEN : PAIRS, :] = new[:, :, at].reshape(2 * GROUP, HEAD_DIM).astype(F32)
        keys_ref[h] = flat[pl.ds(0, SEEN + GROUP, stride=2), :].astype(BF16)
        values_ref[h] = flat[pl.ds(1, SEEN + GROUP, stride=2), :].astype(BF16)

    lax.fori_loop(0, GROUPS, group, 0)
    for g in range(GROUPS):
        moves(g)[1].wait()
    write = pltpu.make_async_copy(new, out_hbm.at[pl.ds(length_ref[0], GROUP)], out_sem.at[GROUPS])
    write.start()
    write.wait()


def shards(
    queries, new_kv, cache, lengths, residual, out_weight, norm_gain, expert_ids, gates, w_gate, w_up, w_down
):
    anywhere = pl.BlockSpec(memory_space=pl.ANY)
    in_vmem = pl.BlockSpec(memory_space=pltpu.VMEM)
    tiles = (EXPERTS, CAP, PIECES, LANES)
    appended, keys, values = pl.pallas_call(
        append_kernel,
        name="append",
        out_shape=(
            jax.ShapeDtypeStruct((CACHE, 2, D), BF16),
            pltpu.VMEM((HEADS, SEEN + GROUP, HEAD_DIM), BF16),
            pltpu.VMEM((HEADS, SEEN + GROUP, HEAD_DIM), BF16),
        ),
        in_specs=[anywhere, anywhere, anywhere],
        out_specs=(anywhere, in_vmem, in_vmem),
        scratch_shapes=[
            pltpu.SMEM((1,), jnp.int32),
            pltpu.VMEM((CACHE, 2, D), BF16),
            pltpu.VMEM((GROUP, 2, D), BF16),
            pltpu.VMEM((HEADS // GROUPS, PAIRS, HEAD_DIM), F32),
            pltpu.SemaphoreType.DMA((GROUPS + 3,)),
            pltpu.SemaphoreType.DMA((GROUPS + 1,)),
        ],
        compiler_params=pltpu.CompilerParams(vmem_limit_bytes=58 * 1024 * 1024),
    )(lengths, new_kv[0], cache[0])
    layer_out = pl.pallas_call(
        layer_kernel,
        name="layer",
        out_shape=pltpu.VMEM((GROUP, D), BF16),
        in_specs=[anywhere] * 5 + [in_vmem, in_vmem] + [anywhere] * 5,
        out_specs=in_vmem,
        scratch_shapes=[
            pltpu.SMEM((1,), jnp.int32),
            pltpu.VMEM((8, SEEN + GROUP), F32),
            pltpu.VMEM((TOP, GROUP), jnp.int32),
            pltpu.VMEM((TOP, GROUP), F32),
            pltpu.VMEM((1, D), F32),
            pltpu.VMEM((GROUP, D), BF16),
            pltpu.VMEM((GROUP, D), BF16),
            pltpu.VMEM((D, D), BF16),
            pltpu.VMEM((2, D, HALF), BF16),
            pltpu.VMEM((2, D, HALF), BF16),
            pltpu.VMEM((2, HALF, D), BF16),
            pltpu.VMEM((GROUP, D), BF16),
            pltpu.VMEM((GROUP, D), F32),
            pltpu.VMEM((GROUP, D), BF16),
            pltpu.VMEM((EXPERTS * CAP, GROUP), BF16),
            pltpu.VMEM((CHUNKS, GROUP, ROWS), BF16),
            pltpu.VMEM((CHUNKS, GROUP, ROWS), BF16),
            pltpu.VMEM((ROWS * PIECES, LANES), F32),
            pltpu.VMEM((BATCH * CAP * PIECES, LANES), F32),
            pltpu.VMEM((BATCH * CAP * PIECES, LANES), F32),
            pltpu.VMEM((ROWS, D), BF16),
            pltpu.VMEM((ROWS, 2 * HALF), BF16),
            pltpu.VMEM(tiles, BF16),
            pltpu.VMEM(tiles, BF16),
            pltpu.VMEM(tiles, BF16),
            pltpu.VMEM(tiles, BF16),
            pltpu.SemaphoreType.DMA((9,)),
            pltpu.SemaphoreType.DMA((GROUPS,)),
            pltpu.SemaphoreType.DMA((3,)),
            pltpu.SemaphoreType.DMA((3,)),
            pltpu.SemaphoreType.DMA((EXPERTS,)),
            pltpu.SemaphoreType.DMA((EXPERTS,)),
            pltpu.SemaphoreType.DMA((EXPERTS,)),
            pltpu.SemaphoreType.DMA((EXPERTS,)),
        ],
        compiler_params=pltpu.CompilerParams(
            collective_id=0, has_side_effects=True, vmem_limit_bytes=58 * 1024 * 1024
        ),
    )(
        lengths,
        expert_ids[0].T,
        gates[0].T,
        norm_gain[None],
        queries[0],
        pltpu.with_memory_space_constraint(keys, pltpu.VMEM),
        pltpu.with_memory_space_constraint(values, pltpu.VMEM),
        residual[0],
        out_weight,
        w_gate[0],
        w_up[0],
        w_down[0],
    )
    return layer_out[None], appended[None]


def solution(mesh):
    shared = ("req", "exp")
    three, four = P(shared, None, None), P(shared, None, None, None)
    return jax.shard_map(
        shards,
        mesh=mesh,
        in_specs=(three, four, four, P(shared), three, P(), P(), three, three, three, three, three),
        out_specs=(three, four),
        check_vma=False,
    )
```
